32 devices in a mesh: tm: 8 (over y, x, core), book: 4 (over z).
Axes of the slice: x: 2, y: 2, z: 4, core: 2. Of those that a mesh axis runs over, the one named last changes fastest.
Arguments:
- q_proj: bfloat16 [16384, 1024], P(('book', 'tm')), parts along dimension 0, may hold values from -52 to 52
- k_proj: bfloat16 [16384, 1024], P(('book', 'tm')), parts along dimension 0, may hold values from -5 to 5
- v_proj: bfloat16 [16384, 1024], P(('book', 'tm')), parts along dimension 0, may hold values from -5 to 5
- gate_bias: float32 [8], replicated, may hold values from -2 to 2
- src_shard: int32 [32, 7], P(('book', 'tm')), parts along dimension 0, may hold values from 0 to 6, as said below
- src_block: int32 [32, 7], P(('book', 'tm')), parts along dimension 0, may hold values from 0 to 3, as said below
- valid: int32 [32, 7], P(('book', 'tm')), parts along dimension 0, may hold values from 0 to 1, as said below
Outputs:
- mixed: bfloat16 [16384, 1024], P(('book', 'tm')), parts along dimension 0
The draws below stay inside these ranges and needn't reach their ends.
There are 4 independent parts, one for each index of `book`. The reference program is written for one: setup_inputs(seed, part) draws one part's arguments, and reference() takes and returns one part's arrays. A program takes and returns all parts, laid end to end along the dimension named above; an argument that names none is the same for every part. Nothing has to cross between parts.
Inputs may be any that keep to these rules, and one draw needn't show every extreme that they name: `src_shard`: in row r the valid entries name distinct segments among r - 7 to r - 1; invalid entries hold 0. `src_block`: invalid entries hold 0. The last segment's list has all 7 entries valid.
All inputs are finite; a program needn't handle non-finite values.
Results may differ from the reference program's by a relative error of at most 0.0033.
Values may be sent and summed in bfloat16 or wider, within the bound.
A program may use at most 64 MiB of HBM per device.

```python
import math
import jax
import jax.numpy as jnp
from jax import lax

SEG = 512
BLOCK = 128
W = 7
HEADS = 8
HD = 128
TOKENS = 4096
N_TM = 8


def request_lists(key):
    base_key = jax.random.fold_in(key, 11)
    row_keys = jax.random.split(jax.random.fold_in(base_key, 1), N_TM)
    orders = jax.vmap(lambda row_key: jax.random.permutation(row_key, W))(row_keys)
    distance = orders.astype(jnp.int32) + 1
    counts = jax.random.randint(jax.random.fold_in(base_key, 2), (N_TM,), 2, W + 1)
    full_reader = N_TM - 1
    readers = jnp.arange(N_TM, dtype=jnp.int32)
    counts = jnp.where(readers == full_reader, W, counts)
    slots = jnp.arange(W, dtype=jnp.int32)
    is_live = (slots[None, :] < counts[:, None]) & (distance <= readers[:, None])
    picked = jax.random.randint(jax.random.fold_in(base_key, 4), (N_TM, W), 0, SEG // BLOCK)
    picked = picked.at[N_TM - 1, 0].set(SEG // BLOCK - 1)
    sources = jnp.where(is_live, readers[:, None] - distance, 0).astype(jnp.int32)
    blocks = jnp.where(is_live, picked, 0).astype(jnp.int32)
    return (sources, blocks, is_live.astype(jnp.int32))


def projections(key):
    feature_count = HEADS * HD
    base_key = jax.random.fold_in(key, 21)
    keys_out = jnp.clip(jax.random.normal(jax.random.fold_in(base_key, 5), (TOKENS, feature_count), jnp.float32), -5.0, 5.0)
    queries_out = jnp.clip(2.0 * jax.random.normal(jax.random.fold_in(base_key, 6), (TOKENS, feature_count), jnp.float32), -10.0, 10.0)
    return (queries_out, keys_out)


def draw_q_proj(key, part):
    return projections(key)[0].astype(jnp.bfloat16)


def draw_k_proj(key, part):
    return projections(key)[1].astype(jnp.bfloat16)


def draw_src_shard(key, part):
    return request_lists(key)[0]


def draw_src_block(key, part):
    return request_lists(key)[1]


def draw_valid(key, part):
    return request_lists(key)[2]


def shard_levels(stream_key, extent, cuts, low, largest):
    loudness, own = 1.0, jax.random.fold_in(stream_key, 6)
    for dim, blocks in cuts:
        steps = jnp.exp(jax.random.uniform(jax.random.fold_in(own, dim), (blocks,), jnp.float32, low / len(cuts), largest / len(cuts)))
        loudness = loudness * jnp.repeat(steps, extent[dim] // blocks).reshape([-1 if axis == dim else 1 for axis in range(len(extent))])
    return loudness


def noise(own_key, extent, width, reach, shards=(), kind=jnp.bfloat16):
    values = jax.random.normal(own_key, extent, jnp.float32) * width
    if len(shards) > 0:
        values = shard_levels(own_key, extent, shards, -0.22, 0.18) * values
    return jnp.clip(values, min=-reach, max=reach).astype(kind)


def setup_inputs(seed: int = 0, part: int = 0) -> dict:
    keys = jax.random.split(jax.random.key(seed), 8)
    part_keys = jax.random.split(jax.random.fold_in(keys[7], part), 8)
    q_proj = draw_q_proj(jax.random.fold_in(jax.random.fold_in(keys[7], part), 71), part)
    k_proj = draw_k_proj(jax.random.fold_in(jax.random.fold_in(keys[7], part), 71), part)
    v_proj = noise(part_keys[2], (TOKENS, HEADS * HD), 1.0, 5.0, ((0, 8),))
    gate_bias = jnp.clip(jax.random.uniform(keys[3], (HEADS,), jnp.float32, -2.0, 2.0), -2.0, 2.0)
    src_shard = draw_src_shard(jax.random.fold_in(jax.random.fold_in(keys[7], part), 71), part)
    src_block = draw_src_block(jax.random.fold_in(jax.random.fold_in(keys[7], part), 71), part)
    valid = draw_valid(jax.random.fold_in(jax.random.fold_in(keys[7], part), 71), part)
    return {"q_proj": q_proj, "k_proj": k_proj, "v_proj": v_proj, "gate_bias": gate_bias, "src_shard": src_shard, "src_block": src_block, "valid": valid}


neg_big = -1e+30

def attend_all(queries, keys_in, values_in, key_mask, scaling):
    scores = jnp.einsum('hqd,hkd->hqk', queries, keys_in, precision=lax.Precision.HIGHEST) * scaling
    scores = jnp.where(key_mask[None], scores, neg_big)
    row_top = lax.optimization_barrier(jnp.max(scores, axis=2, keepdims=True))
    weights = jnp.where(key_mask[None], jnp.exp(scores - row_top), 0.0)
    row_sum = lax.optimization_barrier(jnp.sum(weights, axis=2, keepdims=True))
    rounded = lax.optimization_barrier(weights.astype(jnp.bfloat16)).astype(jnp.float32)
    summed = jnp.einsum('hqk,hkd->hqd', rounded, values_in, precision=lax.Precision.HIGHEST)
    return summed / jnp.maximum(row_sum, 1.0)

def reference(q_proj, k_proj, v_proj, gate_bias, src_shard, src_block, valid):
    model_width = q_proj.shape[1]
    head_count = gate_bias.shape[0]
    head_dim = model_width // head_count
    scaling = 1.0 / math.sqrt(head_dim)
    gate_mix = jax.nn.sigmoid(gate_bias.astype(jnp.float32))[:, None, None]

    def split_heads(matrix):
        return matrix.astype(jnp.float32).reshape(matrix.shape[0], head_count, head_dim).transpose(1, 0, 2)
    rows_at = lax.broadcasted_iota(jnp.int32, (SEG, 2 * SEG), 0)
    cols_at = lax.broadcasted_iota(jnp.int32, (SEG, 2 * SEG), 1)
    offsets = jnp.arange(BLOCK, dtype=jnp.int32)

    def take_rows(matrix, row_start):
        return lax.dynamic_slice_in_dim(matrix, row_start, SEG, 0)

    def one_shard(shard_id):
        row_start = (shard_id * SEG).astype(jnp.int32)
        prev_start = (jnp.maximum(shard_id - 1, 0) * SEG).astype(jnp.int32)
        queries = split_heads(take_rows(q_proj, row_start))
        local_keys = split_heads(jnp.concatenate([take_rows(k_proj, prev_start), take_rows(k_proj, row_start)], axis=0))
        local_values = split_heads(jnp.concatenate([take_rows(v_proj, prev_start), take_rows(v_proj, row_start)], axis=0))
        local_mask = jnp.where(cols_at < SEG, shard_id > 0, cols_at - SEG <= rows_at)
        local_out = attend_all(queries, local_keys, local_values, local_mask, scaling)
        sources = src_shard[shard_id]
        blocks = src_block[shard_id]
        is_live = valid[shard_id] > 0
        token_ids = (sources[:, None] * SEG + blocks[:, None] * BLOCK + offsets[None, :]).reshape(-1).astype(jnp.int32)
        memory_keys = split_heads(jnp.take(k_proj, token_ids, axis=0))
        memory_values = split_heads(jnp.take(v_proj, token_ids, axis=0))
        memory_mask = jnp.broadcast_to(jnp.repeat(is_live, BLOCK)[None, :], (SEG, W * BLOCK))
        memory_out = attend_all(queries, memory_keys, memory_values, memory_mask, scaling)
        mixed_out = gate_mix * memory_out + (1.0 - gate_mix) * local_out
        return mixed_out.transpose(1, 0, 2).reshape(SEG, model_width).astype(jnp.bfloat16)
    shard_ids = jnp.arange(N_TM, dtype=jnp.int32)
    return lax.map(one_shard, shard_ids).reshape(N_TM * SEG, model_width)
```

```python
import functools
import math

import jax
import jax.numpy as jnp
from jax import lax
from jax.experimental import pallas as pl
from jax.experimental.pallas import tpu as pltpu
from jax.sharding import PartitionSpec as P

BLOCK = 128
MASKED = -1e30
FLOOR = -1e29
BARRED = 1e30
UNROLL = 4
GROUPS = ((1, 4), (5, 7))
MESH = pl.DeviceIdType.MESH


def kernel(n, list_len, heads, q_ref, k_ref, v_ref, bias_ref, src_ref, blk_ref, live_ref, out_ref,
           prev_k, prev_v, mem_k, mem_v, send_k, send_v, want_out, want_in,
           top_l, sum_l, acc_l, top_m, sum_m, acc_m,
           relay_k, relay_v, hop_k, hop_v,
           list_ss, list_rs, prev_ss, prev_rs, blk_ss, blk_rs, relay_ss, relay_rs, hop_ss, hop_rs):
    me = lax.axis_index("tm")
    seg, width = q_ref.shape
    hd = width // heads
    per_seg = seg // BLOCK
    far = list_len - 1
    slope = math.log2(math.e) / math.sqrt(hd)

    wants = []
    for d in range(1, list_len + 1):
        want = jnp.int32(-1)
        for e in range(list_len):
            hit = (live_ref[0, e] > 0) & (me - src_ref[0, e] == d)
            want = jnp.where(hit, blk_ref[0, e], want)
        wants.append(want)
        want_out[d - 1] = jnp.full((8, 128), want, jnp.int32)

    def ahead(d):
        return me + d < n

    def behind(d):
        return me - d >= 0

    barrier = pltpu.get_barrier_semaphore()
    for d in range(1, list_len + 1):
        @pl.when(ahead(d))
        def _():
            pl.semaphore_signal(barrier, inc=1, device_id={"tm": me + d}, device_id_type=MESH)

        @pl.when(behind(d))
        def _():
            pl.semaphore_signal(barrier, inc=1, device_id={"tm": me - d}, device_id_type=MESH)
    near = jnp.minimum(me, list_len) + jnp.minimum(n - 1 - me, list_len)
    pl.semaphore_wait(barrier, near)

    detour = n == 8
    odd = lax.rem(me, 2) == 1

    def both(*conditions):
        result = conditions[0]
        for condition in conditions[1:]:
            result = jnp.logical_and(result, condition)
        return result

    def remote(source, target, send, recv, device):
        return pltpu.make_async_remote_copy(source, target, send, recv, device_id={"tm": device},
                                            device_id_type=MESH)

    unfinished = []

    def start(condition, copies):
        @pl.when(condition)
        def _():
            for c in copies():
                c.start()
        unfinished.append((condition, copies))

    def direct(source, d):
        result = both(source >= 0, source + d < n)
        if d == 2:
            result = both(result, lax.rem(source, 2) == 0)
        if detour and d in (3, 4):
            result = both(result, source != 3)
        return result

    def list_copy(d, target, slot=None):
        slot = d - 1 if slot is None else slot
        return [remote(want_out.at[d - 1], want_in.at[slot], list_ss.at[d - 1], list_rs.at[slot], target)]

    def pieces(keys, values):
        half = seg // 2
        return [part.at[pl.ds(i * half, half)] for part in (keys, values) for i in range(2)]

    def prev_copies(keys, values, target, chosen=range(4)):
        return [remote(pieces(keys, values)[i], pieces(prev_k, prev_v)[i], prev_ss.at[i], prev_rs.at[i], target)
                for i in chosen]

    def relay_copies(chosen=range(4)):
        return [remote(pieces(k_ref, v_ref)[i], pieces(relay_k, relay_v)[i], relay_ss.at[i], relay_rs.at[i], 7)
                for i in chosen]

    def block_copies(d, target, slot=None):
        slot = d - 2 if slot is None else slot
        return [remote(here.at[slot], there.at[d - 1], blk_ss.at[i, slot], blk_rs.at[i, d - 2], target)
                for i, (here, there) in enumerate(((send_k, mem_k), (send_v, mem_v)))]

    def hop_in(d):
        return [remote(here.at[d - 2], there, blk_ss.at[i, d - 2], hop_rs.at[i], d - 2)
                for i, (here, there) in enumerate(((send_k, hop_k), (send_v, hop_v)))]

    def hop_out(d):
        return [remote(here, there.at[d - 1], hop_ss.at[i], blk_rs.at[i, d - 2], d)
                for i, (here, there) in enumerate(((hop_k, mem_k), (hop_v, mem_v)))]

    def pick(want, from_k, from_v, to_k, to_v):
        ones = [jnp.where(want == b, 1.0, 0.0)[:1].astype(jnp.bfloat16) for b in range(per_seg)]

        def one_strip(h, carry):
            cols = pl.ds(pl.multiple_of(h * 128, 128), 128)
            for source, target in ((from_k, to_k), (from_v, to_v)):
                total = source[:BLOCK, cols] * ones[0]
                for b in range(1, per_seg):
                    total = total + source[b * BLOCK:(b + 1) * BLOCK, cols] * ones[b]
                target[:, cols] = total
            return carry

        lax.fori_loop(0, width // 128, one_strip, 0)

    for d in range(list_len, 1, -1):
        start(direct(me - d, d), lambda d=d: list_copy(d, me - d))
    start(both(odd, behind(2)), lambda: list_copy(2, me - 1, list_len))
    if detour:
        start(me == 6, lambda: list_copy(3, 7))
        start(me == 3, relay_copies)
        start(both(ahead(1), me != 3), lambda: prev_copies(k_ref, v_ref, me + 1))
    else:
        start(ahead(1), lambda: prev_copies(k_ref, v_ref, me + 1))

    for d in range(list_len, 1, -1):
        @pl.when(direct(me, d))
        def _():
            for c in list_copy(d, me + d):
                c.wait_recv()
            pick(want_in[d - 1], k_ref, v_ref, send_k.at[d - 2], send_v.at[d - 2])
    for d in range(list_len, 1, -1):
        if detour and d in (6, 7):
            start(me == 0, lambda d=d: hop_in(d))
            start(both(direct(me, d), me != 0), lambda d=d: block_copies(d, me + d))
        else:
            start(direct(me, d), lambda d=d: block_copies(d, me + d))

    def absorb(load_k, load_v, top, total, acc, some_wants=None, causal=False, first=False):
        lives = None if some_wants is None else [jnp.full((1, seg), w, jnp.int32) >= 0 for w in some_wants]

        def one_head(h, carry):
            cols = pl.ds(pl.multiple_of(h * hd, hd), hd)
            row = pl.ds(h, 1)
            s = lax.dot_general(load_k(cols), q_ref[:, cols], (((1,), (1,)), ((), ())),
                                preferred_element_type=jnp.float32)
            if causal:
                key_at = lax.broadcasted_iota(jnp.int32, s.shape, 0)
                query_at = lax.broadcasted_iota(jnp.int32, s.shape, 1)
                s = jnp.where(key_at <= query_at, s, MASKED)
            new = None if first else top[row, :]
            if lives is None:
                high = jnp.max(s, axis=0, keepdims=True)
                new = high if first else jnp.maximum(new, high)
                p = jnp.exp2((s - new) * slope)
            else:
                strips = [s[i * BLOCK:(i + 1) * BLOCK] for i in range(len(lives))]
                for strip, live in zip(strips, lives):
                    high = jnp.where(live, jnp.max(strip, axis=0, keepdims=True), FLOOR)
                    new = high if new is None else jnp.maximum(new, high)
                p = jnp.concatenate([jnp.exp2((strip - jnp.where(live, new, BARRED)) * slope)
                                     for strip, live in zip(strips, lives)], axis=0)
            part = jnp.sum(p, axis=0, keepdims=True)
            mixed = lax.dot_general(load_v(cols), p.astype(jnp.bfloat16), (((0,), (0,)), ((), ())),
                                    preferred_element_type=jnp.float32)
            if first:
                total[row, :] = part
                acc[cols, :] = mixed
            else:
                shrink = jnp.exp2((top[row, :] - new) * slope)
                total[row, :] = total[row, :] * shrink + part
                acc[cols, :] = acc[cols, :] * shrink + mixed
            top[row, :] = new
            return carry

        lax.fori_loop(0, heads, one_head, 0, unroll=UNROLL)

    @pl.when(jnp.logical_not(behind(1)))
    def _():
        sum_m[...] = jnp.zeros_like(sum_m)
        acc_m[...] = jnp.zeros_like(acc_m)
    for d in range(2, list_len + 1):
        @pl.when(jnp.logical_not(behind(d)))
        def _():
            mem_k[d - 1] = jnp.zeros((BLOCK, width), jnp.bfloat16)
            mem_v[d - 1] = jnp.zeros((BLOCK, width), jnp.bfloat16)

    absorb(lambda c: k_ref[:, c], lambda c: v_ref[:, c], top_l, sum_l, acc_l, causal=True, first=True)

    if detour:
        for d in (6, 7):
            @pl.when(me == d - 2)
            def _():
                for c in hop_in(d):
                    c.wait_recv()
            start(me == d - 2, lambda d=d: hop_out(d))

        def forward(i):
            @pl.when(me == 7)
            def _():
                relay_copies([i])[0].wait_recv()
            start(me == 7, lambda: prev_copies(relay_k, relay_v, 4, [i]))

        forward(0)

    def take_prev():
        for c in prev_copies(k_ref, v_ref, me - 1):
            c.wait_recv()

    pl.when(behind(1))(take_prev)
    pass_on = both(jnp.logical_not(odd), behind(1), ahead(1))

    @pl.when(pass_on)
    def _():
        list_copy(2, me, list_len)[0].wait_recv()
        pick(want_in[list_len], prev_k, prev_v, send_k.at[far], send_v.at[far])
    start(pass_on, lambda: block_copies(2, me + 1, far))

    @pl.when(behind(1))
    def _():
        absorb(lambda c: prev_k[:, c], lambda c: prev_v[:, c], top_l, sum_l, acc_l)
        pick(want_out[0], prev_k, prev_v, mem_k.at[0], mem_v.at[0])

    if detour:
        for i in range(1, 4):
            forward(i)

        @pl.when(me == 7)
        def _():
            list_copy(3, 6)[0].wait_recv()
            pick(want_in[2], relay_k, relay_v, send_k.at[1], send_v.at[1])
            pick(want_out[3], relay_k, relay_v, mem_k.at[3], mem_v.at[3])
        start(me == 7, lambda: block_copies(3, 6))

    for low, high in GROUPS:
        for d in range(max(low, 2), min(high, list_len) + 1):
            @pl.when(both(behind(d), me != 7) if detour and d == 4 else behind(d))
            def _():
                for c in block_copies(d, me - d):
                    c.wait_recv()

        @pl.when(behind(low))
        def _():
            last = min(high, list_len)

            def load(blocks):
                return lambda c: blocks[low - 1:last, :, c].reshape((last - low + 1) * BLOCK, hd)
            absorb(load(mem_k), load(mem_v), top_m, sum_m, acc_m, some_wants=wants[low - 1:last], first=low == 1)

    def finish(h, carry):
        cols = pl.ds(pl.multiple_of(h * hd, hd), hd)
        row = pl.ds(h, 1)
        gate = 1.0 / (1.0 + jnp.exp(jnp.full((1, seg), -bias_ref[h], jnp.float32)))
        mixed = (acc_m[cols, :] * (gate / jnp.maximum(sum_m[row, :], 1.0))
                 + acc_l[cols, :] * ((1.0 - gate) / jnp.maximum(sum_l[row, :], 1.0)))
        out_ref[:, cols] = mixed.T.astype(jnp.bfloat16)
        return carry

    lax.fori_loop(0, heads, finish, 0, unroll=UNROLL)

    for condition, copies in unfinished:
        @pl.when(condition)
        def _():
            for c in copies():
                c.wait_send()


ORDER = ((0, 0, 0, 0, 0, 0, 0),
         (1, 0, 0, 0, 0, 0, 0),
         (1, 0, 0, 0, 0, 0, 2),
         (1, 2, 0, 0, 0, 0, 3),
         (4, 1, 0, 0, 0, 3, 2),
         (1, 5, 2, 0, 0, 3, 4),
         (1, 3, 2, 4, 0, 6, 5),
         (1, 4, 2, 3, 5, 6, 7))
STAGES = ((0, 3), (3, 2), (5, 1), (6, 1))
HOLDERS = ((), (), (0,), (0, 2), (1, 2), (1, 2, 4), (1, 2, 4, 7), (1, 2, 4, 6))
SENDS = {0: ((2, 2, "own"), (3, 3, "own")),
         1: ((7, 6, "own"), (6, 5, "own"), (4, 3, "own"), (5, 4, "own")),
         2: ((5, 3, "own"), (4, 2, "own"), (6, 4, "own"), (7, 5, "own"), (3, 2, "prev")),
         4: ((6, 2, "own"), (7, 3, "own"), (6, 6, "aux"), (7, 7, "aux"), (5, 5, "aux"), (5, 2, "prev")),
         6: ((7, 2, "prev"),),
         7: ((6, 3, "aux"),)}
SLOTS = 6
VMEM_LIMIT = 60 * 2 ** 20


def eight(list_len, heads, q_hbm, k_hbm, v_hbm, bias_hbm, src_hbm, blk_hbm, live_hbm, out_ref,
          q_ref, k_ref, v_ref, bias_ref, src_ref, blk_ref, live_ref, load_s, prev_k, prev_v, aux_k, aux_v, mem_k, mem_v, send_k, send_v, want_out, want_in,
          top_l, sum_l, acc_l, top_m, sum_m, acc_m,
          list_ss, list_rs, prev_ss, prev_rs, aux_ss, aux_rs, blk_ss, blk_rs):
    me = lax.axis_index("tm")
    seg, width = q_ref.shape
    hd = width // heads
    per_seg = seg // BLOCK
    loads = [pltpu.make_async_copy(source, target, load_s.at[i]) for i, (source, target) in enumerate(
        ((src_hbm, src_ref), (blk_hbm, blk_ref), (live_hbm, live_ref), (bias_hbm, bias_ref),
         (k_hbm, k_ref), (q_hbm, q_ref), (v_hbm, v_ref)))]
    for load in loads:
        load.start()
    barrier = pltpu.get_barrier_semaphore()
    for other in range(8):
        @pl.when(me != other)
        def _():
            pl.semaphore_signal(barrier, inc=1, device_id={"tm": other}, device_id_type=MESH)
    places = len(ORDER[0])
    slope = math.log2(math.e) / math.sqrt(hd)

    def any_of(devices):
        result = me == devices[0]
        for device in devices[1:]:
            result = jnp.logical_or(result, me == device)
        return result

    def want_of(distance):
        want = jnp.int32(-1)
        for e in range(list_len):
            hit = (live_ref[0, e] > 0) & (me - src_ref[0, e] == distance)
            want = jnp.where(hit, blk_ref[0, e], want)
        return want

    for load in loads[:3]:
        load.wait()
    wants = []
    for p in range(places):
        distance = jnp.int32(100)
        for r in range(8):
            if ORDER[r][p]:
                distance = jnp.where(me == r, ORDER[r][p], distance)
        wants.append(want_of(distance))
    row = lax.broadcasted_iota(jnp.int32, (8, 128), 0)
    tile = jnp.full((8, 128), -1, jnp.int32)
    for d in range(1, list_len + 1):
        tile = jnp.where(row == d - 1, want_of(d), tile)
    want_out[...] = tile
    pl.semaphore_wait(barrier, 7)

    def remote(source, target, send, recv, device):
        return pltpu.make_async_remote_copy(source, target, send, recv, device_id={"tm": device},
                                            device_id_type=MESH)

    def pieces(keys, values):
        half = width // 2
        return [part.at[:, pl.ds(i * half, half)] for i in range(2) for part in (keys, values)]

    def prev_copy(i, keys, values, device):
        return remote(pieces(keys, values)[i], pieces(prev_k, prev_v)[i], prev_ss.at[i], prev_rs.at[i], device)

    def aux_copy(i, device):
        return remote(pieces(k_hbm, v_hbm)[i], pieces(aux_k, aux_v)[i], aux_ss.at[i], aux_rs.at[i], device)

    def list_copy(i, slot, device):
        return remote(want_out, want_in.at[slot], list_ss.at[i], list_rs.at[slot], device)

    def block_copies(slot, place, device):
        return [remote(here.at[slot], there.at[place], blk_ss.at[i, slot], blk_rs.at[i, place], device)
                for i, (here, there) in enumerate(((send_k, mem_k), (send_v, mem_v)))]

    def pick(want, source, to_k, to_v):
        from_k, from_v = {"own": (k_ref, v_ref), "prev": (prev_k, prev_v), "aux": (aux_k, aux_v)}[source]
        ones = [jnp.where(want == b, 1.0, 0.0).astype(jnp.bfloat16) for b in range(per_seg)]

        def one_strip(h, carry):
            cols = pl.ds(pl.multiple_of(h * 128, 128), 128)
            for origin, target in ((from_k, to_k), (from_v, to_v)):
                total = origin[:BLOCK, cols] * ones[0]
                for b in range(1, per_seg):
                    total = total + origin[b * BLOCK:(b + 1) * BLOCK, cols] * ones[b]
                target[:, cols] = total
            return carry

        lax.fori_loop(0, width // 128, one_strip, 0)

    def pick_send(device, chosen):
        for slot in chosen:
            reader, distance, source = SENDS[device][slot]
            pick(want_in[reader - 2, distance - 1:distance, :], source, send_k.at[slot], send_v.at[slot])

    def start_send(device, chosen):
        for slot in chosen:
            reader, distance, source = SENDS[device][slot]
            for c in block_copies(slot, ORDER[reader].index(distance), reader):
                c.start()

    def pick_own(place, source):
        pick(jnp.full((1, 128), wants[place], jnp.int32), source, mem_k.at[place], mem_v.at[place])

    @pl.when(me == 3)
    def _():
        for i in range(4):
            aux_copy(i, 7).start()

    @pl.when(me == 0)
    def _():
        for i in range(4):
            aux_copy(i, 4).start()
    for r in range(2, 8):
        @pl.when(me == r)
        def _():
            for i, holder in enumerate(HOLDERS[r]):
                list_copy(i, r - 2, holder).start()
    gives = any_of((0, 1, 2, 4, 5, 6))

    @pl.when(gives)
    def _():
        for i in range(4):
            prev_copy(i, k_hbm, v_hbm, me + 1).start()

    for load in loads[3:]:
        load.wait()

    for device in (0, 1, 2, 4, 6, 7):
        @pl.when(me == device)
        def _():
            for r in range(2, 8):
                if device in HOLDERS[r]:
                    list_copy(0, r - 2, r).wait_recv()
            pick_send(device, [i for i, entry in enumerate(SENDS[device]) if entry[2] == "own"])
            if device == 1:
                start_send(1, (0, 1))

    for devices, place in (((1, 2), 1), ((1, 2, 3, 4), 2), ((6,), 4)):
        @pl.when(any_of(devices))
        def _():
            mem_k[place] = jnp.zeros((BLOCK, width), jnp.bfloat16)
            mem_v[place] = jnp.zeros((BLOCK, width), jnp.bfloat16)

    def absorb(load_k, load_v, top, total, acc, some_wants=None, causal=False, first=False):
        lives = None if some_wants is None else [jnp.full((1, seg), w, jnp.int32) >= 0 for w in some_wants]

        def one_head(h, carry):
            cols = pl.ds(pl.multiple_of(h * hd, hd), hd)
            row = pl.ds(h, 1)
            s = lax.dot_general(load_k(cols), q_ref[:, cols], (((1,), (1,)), ((), ())),
                                preferred_element_type=jnp.float32)
            if causal:
                key_at = lax.broadcasted_iota(jnp.int32, s.shape, 0)
                query_at = lax.broadcasted_iota(jnp.int32, s.shape, 1)
                s = jnp.where(key_at <= query_at, s, MASKED)
            new = None if first else top[row, :]
            if lives is None:
                high = jnp.max(s, axis=0, keepdims=True)
                new = high if first else jnp.maximum(new, high)
                p = jnp.exp2((s - new) * slope)
            else:
                strips = [s[i * BLOCK:(i + 1) * BLOCK] for i in range(len(lives))]
                for strip, live in zip(strips, lives):
                    high = jnp.where(live, jnp.max(strip, axis=0, keepdims=True), FLOOR)
                    new = high if new is None else jnp.maximum(new, high)
                p = jnp.concatenate([jnp.exp2((strip - jnp.where(live, new, BARRED)) * slope)
                                     for strip, live in zip(strips, lives)], axis=0)
            part = jnp.sum(p, axis=0, keepdims=True)
            mixed = lax.dot_general(load_v(cols), p.astype(jnp.bfloat16), (((0,), (0,)), ((), ())),
                                    preferred_element_type=jnp.float32)
            if first:
                total[row, :] = part
                acc[cols, :] = mixed
            else:
                shrink = jnp.exp2((top[row, :] - new) * slope)
                total[row, :] = total[row, :] * shrink + part
                acc[cols, :] = acc[cols, :] * shrink + mixed
            top[row, :] = new
            return carry

        lax.fori_loop(0, heads, one_head, 0, unroll=UNROLL)

    @pl.when(me == 0)
    def _():
        sum_m[...] = jnp.zeros_like(sum_m)
        acc_m[...] = jnp.zeros_like(acc_m)

    absorb(lambda c: k_ref[:, c], lambda c: v_ref[:, c], top_l, sum_l, acc_l, causal=True, first=True)

    def forward(i):
        @pl.when(me == 7)
        def _():
            aux_copy(i, 3).wait_recv()
            prev_copy(i, aux_k, aux_v, 4).start()

    def take_prev(chosen):
        for i in chosen:
            prev_copy(i, k_hbm, v_hbm, 0).wait_recv()

    def take_aux(chosen):
        for i in chosen:
            aux_copy(i, 0).wait_recv()

    forward(0)

    @pl.when(me == 0)
    def _():
        for i in range(4):
            aux_copy(i, 4).wait_send()
        start_send(0, (0, 1))

    @pl.when(me == 2)
    def _():
        take_prev(range(4))
        start_send(2, (0, 1, 2, 3))

    @pl.when(me == 4)
    def _():
        take_aux(range(4))
        start_send(4, (0, 1))
        pick_send(4, (2, 3, 4))
        start_send(4, (2, 3, 4))
        pick_own(0, "aux")

    @pl.when(me == 2)
    def _():
        pick_send(2, [4])
        start_send(2, [4])

    @pl.when(any_of((1, 3, 4, 5, 6, 7)))
    def _():
        take_prev(range(4))

    @pl.when(me == 4)
    def _():
        pick_send(4, [5])
        start_send(4, [5])
        pick_own(1, "prev")

    @pl.when(me == 6)
    def _():
        pick_send(6, [0])
        start_send(6, [0])

    @pl.when(any_of((1, 2, 3, 5, 6, 7)))
    def _():
        pick_own(0, "prev")

    @pl.when(me >= 1)
    def _():
        absorb(lambda c: prev_k[:, c], lambda c: prev_v[:, c], top_l, sum_l, acc_l)

    @pl.when(me == 1)
    def _():
        for i in range(4):
            prev_copy(i, k_hbm, v_hbm, 2).wait_send()
        start_send(1, (2, 3))

    for i in range(1, 4):
        forward(i)

    @pl.when(me == 7)
    def _():
        pick_send(7, [0])
        start_send(7, [0])
        pick_own(1, "aux")

    remote_places = {r: [] for r in range(8)}
    for device, entries in SENDS.items():
        for reader, distance, source in entries:
            remote_places[reader].append(ORDER[reader].index(distance))

    for low, count in STAGES:
        for place in range(low, low + count):
            readers = [r for r in range(8) if place in remote_places[r]]
            if readers:
                @pl.when(any_of(readers))
                def _():
                    for c in block_copies(0, place, 0):
                        c.wait_recv()
        users = [r for r in range(8) if any(ORDER[r][low:low + count])]

        @pl.when(any_of(users))
        def _():
            def load(blocks):
                return lambda c: blocks[low:low + count, :, c].reshape(count * BLOCK, hd)
            absorb(load(mem_k), load(mem_v), top_m, sum_m, acc_m, some_wants=wants[low:low + count],
                   first=low == 0)

    def finish(h, carry):
        cols = pl.ds(pl.multiple_of(h * hd, hd), hd)
        row = pl.ds(h, 1)
        gate = 1.0 / (1.0 + jnp.exp(jnp.full((1, seg), -bias_ref[h], jnp.float32)))
        mixed = (acc_m[cols, :] * (gate / jnp.maximum(sum_m[row, :], 1.0))
                 + acc_l[cols, :] * ((1.0 - gate) / jnp.maximum(sum_l[row, :], 1.0)))
        out_ref[:, cols] = mixed.T.astype(jnp.bfloat16)
        return carry

    lax.fori_loop(0, heads, finish, 0, unroll=UNROLL)

    for device in range(8):
        @pl.when(me == device)
        def _():
            for i in range(len(HOLDERS[device])):
                list_copy(i, 0, 0).wait_send()
            for slot in range(len(SENDS.get(device, ()))):
                for c in block_copies(slot, 0, 0):
                    c.wait_send()
            if device == 3:
                for i in range(4):
                    aux_copy(i, 4).wait_send()
            if device not in (1, 3):
                for i in range(4):
                    prev_copy(i, k_hbm, v_hbm, 2).wait_send()


def general(n, q_proj, k_proj, v_proj, gate_bias, src_shard, src_block, valid):
    seg, width = q_proj.shape
    heads = gate_bias.shape[0]
    list_len = src_shard.shape[1]
    far = list_len - 1
    vmem = pl.BlockSpec(memory_space=pltpu.VMEM)
    smem = pl.BlockSpec(memory_space=pltpu.SMEM)
    return pl.pallas_call(
        functools.partial(kernel, n, list_len, heads),
        out_shape=jax.ShapeDtypeStruct((seg, width), jnp.bfloat16),
        in_specs=[vmem] * 3 + [smem] * 4,
        out_specs=vmem,
        scratch_shapes=[
            pltpu.VMEM((seg, width), jnp.bfloat16),
            pltpu.VMEM((seg, width), jnp.bfloat16),
            pltpu.VMEM((list_len, BLOCK, width), jnp.bfloat16),
            pltpu.VMEM((list_len, BLOCK, width), jnp.bfloat16),
            pltpu.VMEM((far + 1, BLOCK, width), jnp.bfloat16),
            pltpu.VMEM((far + 1, BLOCK, width), jnp.bfloat16),
            pltpu.VMEM((list_len, 8, 128), jnp.int32),
            pltpu.VMEM((list_len + 1, 8, 128), jnp.int32),
            pltpu.VMEM((heads, seg), jnp.float32),
            pltpu.VMEM((heads, seg), jnp.float32),
            pltpu.VMEM((width, seg), jnp.float32),
            pltpu.VMEM((heads, seg), jnp.float32),
            pltpu.VMEM((heads, seg), jnp.float32),
            pltpu.VMEM((width, seg), jnp.float32),
            pltpu.VMEM((seg, width), jnp.bfloat16),
            pltpu.VMEM((seg, width), jnp.bfloat16),
            pltpu.VMEM((BLOCK, width), jnp.bfloat16),
            pltpu.VMEM((BLOCK, width), jnp.bfloat16),
            pltpu.SemaphoreType.DMA((list_len,)),
            pltpu.SemaphoreType.DMA((list_len + 1,)),
            pltpu.SemaphoreType.DMA((4,)),
            pltpu.SemaphoreType.DMA((4,)),
            pltpu.SemaphoreType.DMA((2, far + 1)),
            pltpu.SemaphoreType.DMA((2, far)),
            pltpu.SemaphoreType.DMA((4,)),
            pltpu.SemaphoreType.DMA((4,)),
            pltpu.SemaphoreType.DMA((2,)),
            pltpu.SemaphoreType.DMA((2,)),
        ],
        compiler_params=pltpu.CompilerParams(collective_id=0, has_side_effects=True),
    )(q_proj, k_proj, v_proj, gate_bias, src_shard, src_block, valid)


def shards(n, q_proj, k_proj, v_proj, gate_bias, src_shard, src_block, valid):
    seg, width = q_proj.shape
    heads = gate_bias.shape[0]
    list_len = src_shard.shape[1]
    vmem = pl.BlockSpec(memory_space=pltpu.VMEM)
    if n != 8:
        return general(n, q_proj, k_proj, v_proj, gate_bias, src_shard, src_block, valid)
    whole = pltpu.VMEM((seg, width), jnp.bfloat16)
    return pl.pallas_call(
        functools.partial(eight, list_len, heads),
        out_shape=jax.ShapeDtypeStruct((seg, width), jnp.bfloat16),
        in_specs=[pl.BlockSpec(memory_space=pltpu.HBM)] * 7,
        out_specs=vmem,
        scratch_shapes=[whole] * 3 + [pltpu.SMEM(gate_bias.shape, jnp.float32)]
        + [pltpu.SMEM(src_shard.shape, jnp.int32)] * 3 + [pltpu.SemaphoreType.DMA((7,))] + [whole] * 4
        + [pltpu.VMEM((len(ORDER[0]), BLOCK, width), jnp.bfloat16)] * 2
        + [pltpu.VMEM((SLOTS, BLOCK, width), jnp.bfloat16)] * 2
        + [pltpu.VMEM((8, 128), jnp.int32), pltpu.VMEM((6, 8, 128), jnp.int32)]
        + [pltpu.VMEM((heads, seg), jnp.float32), pltpu.VMEM((heads, seg), jnp.float32),
           pltpu.VMEM((width, seg), jnp.float32)] * 2
        + [pltpu.SemaphoreType.DMA((4,)), pltpu.SemaphoreType.DMA((6,))]
        + [pltpu.SemaphoreType.DMA((4,))] * 4
        + [pltpu.SemaphoreType.DMA((2, SLOTS)), pltpu.SemaphoreType.DMA((2, len(ORDER[0])))],
        compiler_params=pltpu.CompilerParams(collective_id=0, has_side_effects=True,
                                             vmem_limit_bytes=VMEM_LIMIT),
    )(q_proj, k_proj, v_proj, gate_bias, src_shard, src_block, valid)


def solution(mesh):
    rows = P(("book", "tm"), None)
    return jax.shard_map(functools.partial(shards, mesh.shape["tm"]), mesh=mesh,
                         in_specs=(rows, rows, rows, P(), rows, rows, rows), out_specs=rows, check_vma=False)
```

```python
import functools
import math

import jax
import jax.numpy as jnp
from jax import lax
from jax.experimental import pallas as pl
from jax.experimental.pallas import tpu as pltpu
from jax.sharding import PartitionSpec as P

BLOCK = 128
MASKED = -1e30
FLOOR = -1e29
BARRED = 1e30
UNROLL = 4
GROUPS = ((1, 4), (5, 7))
MESH = pl.DeviceIdType.MESH


def kernel(n, list_len, heads, q_ref, k_ref, v_ref, bias_ref, src_ref, blk_ref, live_ref, out_ref,
           prev_k, prev_v, mem_k, mem_v, send_k, send_v, want_out, want_in,
           top_l, sum_l, acc_l, top_m, sum_m, acc_m,
           relay_k, relay_v, hop_k, hop_v,
           list_ss, list_rs, prev_ss, prev_rs, blk_ss, blk_rs, relay_ss, relay_rs, hop_ss, hop_rs):
    me = lax.axis_index("tm")
    seg, width = q_ref.shape
    hd = width // heads
    per_seg = seg // BLOCK
    far = list_len - 1
    slope = math.log2(math.e) / math.sqrt(hd)

    wants = []
    for d in range(1, list_len + 1):
        want = jnp.int32(-1)
        for e in range(list_len):
            hit = (live_ref[0, e] > 0) & (me - src_ref[0, e] == d)
            want = jnp.where(hit, blk_ref[0, e], want)
        wants.append(want)
        want_out[d - 1] = jnp.full((8, 128), want, jnp.int32)

    def ahead(d):
        return me + d < n

    def behind(d):
        return me - d >= 0

    barrier = pltpu.get_barrier_semaphore()
    for d in range(1, list_len + 1):
        @pl.when(ahead(d))
        def _():
            pl.semaphore_signal(barrier, inc=1, device_id={"tm": me + d}, device_id_type=MESH)

        @pl.when(behind(d))
        def _():
            pl.semaphore_signal(barrier, inc=1, device_id={"tm": me - d}, device_id_type=MESH)
    near = jnp.minimum(me, list_len) + jnp.minimum(n - 1 - me, list_len)
    pl.semaphore_wait(barrier, near)

    detour = n == 8
    odd = lax.rem(me, 2) == 1

    def both(*conditions):
        result = conditions[0]
        for condition in conditions[1:]:
            result = jnp.logical_and(result, condition)
        return result

    def remote(source, target, send, recv, device):
        return pltpu.make_async_remote_copy(source, target, send, recv, device_id={"tm": device},
                                            device_id_type=MESH)

    unfinished = []

    def start(condition, copies):
        @pl.when(condition)
        def _():
            for c in copies():
                c.start()
        unfinished.append((condition, copies))

    def direct(source, d):
        result = both(source >= 0, source + d < n)
        if d == 2:
            result = both(result, lax.rem(source, 2) == 0)
        if detour and d in (3, 4):
            result = both(result, source != 3)
        return result

    def list_copy(d, target, slot=None):
        slot = d - 1 if slot is None else slot
        return [remote(want_out.at[d - 1], want_in.at[slot], list_ss.at[d - 1], list_rs.at[slot], target)]

    def pieces(keys, values):
        half = seg // 2
        return [part.at[pl.ds(i * half, half)] for part in (keys, values) for i in range(2)]

    def prev_copies(keys, values, target, chosen=range(4)):
        return [remote(pieces(keys, values)[i], pieces(prev_k, prev_v)[i], prev_ss.at[i], prev_rs.at[i], target)
                for i in chosen]

    def relay_copies(chosen=range(4)):
        return [remote(pieces(k_ref, v_ref)[i], pieces(relay_k, relay_v)[i], relay_ss.at[i], relay_rs.at[i], 7)
                for i in chosen]

    def block_copies(d, target, slot=None):
        slot = d - 2 if slot is None else slot
        return [remote(here.at[slot], there.at[d - 1], blk_ss.at[i, slot], blk_rs.at[i, d - 2], target)
                for i, (here, there) in enumerate(((send_k, mem_k), (send_v, mem_v)))]

    def hop_in(d):
        return [remote(here.at[d - 2], there, blk_ss.at[i, d - 2], hop_rs.at[i], d - 2)
                for i, (here, there) in enumerate(((send_k, hop_k), (send_v, hop_v)))]

    def hop_out(d):
        return [remote(here, there.at[d - 1], hop_ss.at[i], blk_rs.at[i, d - 2], d)
                for i, (here, there) in enumerate(((hop_k, mem_k), (hop_v, mem_v)))]

    def pick(want, from_k, from_v, to_k, to_v):
        ones = [jnp.where(want == b, 1.0, 0.0)[:1].astype(jnp.bfloat16) for b in range(per_seg)]

        def one_strip(h, carry):
            cols = pl.ds(pl.multiple_of(h * 128, 128), 128)
            for source, target in ((from_k, to_k), (from_v, to_v)):
                total = source[:BLOCK, cols] * ones[0]
                for b in range(1, per_seg):
                    total = total + source[b * BLOCK:(b + 1) * BLOCK, cols] * ones[b]
                target[:, cols] = total
            return carry

        lax.fori_loop(0, width // 128, one_strip, 0)

    for d in range(list_len, 1, -1):
        start(direct(me - d, d), lambda d=d: list_copy(d, me - d))
    start(both(odd, behind(2)), lambda: list_copy(2, me - 1, list_len))
    if detour:
        start(me == 6, lambda: list_copy(3, 7))
        start(me == 3, relay_copies)
        start(both(ahead(1), me != 3), lambda: prev_copies(k_ref, v_ref, me + 1))
    else:
        start(ahead(1), lambda: prev_copies(k_ref, v_ref, me + 1))

    for d in range(list_len, 1, -1):
        @pl.when(direct(me, d))
        def _():
            for c in list_copy(d, me + d):
                c.wait_recv()
            pick(want_in[d - 1], k_ref, v_ref, send_k.at[d - 2], send_v.at[d - 2])
    for d in range(list_len, 1, -1):
        if detour and d in (6, 7):
            start(me == 0, lambda d=d: hop_in(d))
            start(both(direct(me, d), me != 0), lambda d=d: block_copies(d, me + d))
        else:
            start(direct(me, d), lambda d=d: block_copies(d, me + d))

    def absorb(load_k, load_v, top, total, acc, some_wants=None, causal=False, first=False):
        lives = None if some_wants is None else [jnp.full((1, seg), w, jnp.int32) >= 0 for w in some_wants]

        def one_head(h, carry):
            cols = pl.ds(pl.multiple_of(h * hd, hd), hd)
            row = pl.ds(h, 1)
            s = lax.dot_general(load_k(cols), q_ref[:, cols], (((1,), (1,)), ((), ())),
                                preferred_element_type=jnp.float32)
            if causal:
                key_at = lax.broadcasted_iota(jnp.int32, s.shape, 0)
                query_at = lax.broadcasted_iota(jnp.int32, s.shape, 1)
                s = jnp.where(key_at <= query_at, s, MASKED)
            new = None if first else top[row, :]
            if lives is None:
                high = jnp.max(s, axis=0, keepdims=True)
                new = high if first else jnp.maximum(new, high)
                p = jnp.exp2((s - new) * slope)
            else:
                strips = [s[i * BLOCK:(i + 1) * BLOCK] for i in range(len(lives))]
                for strip, live in zip(strips, lives):
                    high = jnp.where(live, jnp.max(strip, axis=0, keepdims=True), FLOOR)
                    new = high if new is None else jnp.maximum(new, high)
                p = jnp.concatenate([jnp.exp2((strip - jnp.where(live, new, BARRED)) * slope)
                                     for strip, live in zip(strips, lives)], axis=0)
            part = jnp.sum(p, axis=0, keepdims=True)
            mixed = lax.dot_general(load_v(cols), p.astype(jnp.bfloat16), (((0,), (0,)), ((), ())),
                                    preferred_element_type=jnp.float32)
            if first:
                total[row, :] = part
                acc[cols, :] = mixed
            else:
                shrink = jnp.exp2((top[row, :] - new) * slope)
                total[row, :] = total[row, :] * shrink + part
                acc[cols, :] = acc[cols, :] * shrink + mixed
            top[row, :] = new
            return carry

        lax.fori_loop(0, heads, one_head, 0, unroll=UNROLL)

    @pl.when(jnp.logical_not(behind(1)))
    def _():
        sum_m[...] = jnp.zeros_like(sum_m)
        acc_m[...] = jnp.zeros_like(acc_m)
    for d in range(2, list_len + 1):
        @pl.when(jnp.logical_not(behind(d)))
        def _():
            mem_k[d - 1] = jnp.zeros((BLOCK, width), jnp.bfloat16)
            mem_v[d - 1] = jnp.zeros((BLOCK, width), jnp.bfloat16)

    absorb(lambda c: k_ref[:, c], lambda c: v_ref[:, c], top_l, sum_l, acc_l, causal=True, first=True)

    if detour:
        for d in (6, 7):
            @pl.when(me == d - 2)
            def _():
                for c in hop_in(d):
                    c.wait_recv()
            start(me == d - 2, lambda d=d: hop_out(d))

        def forward(i):
            @pl.when(me == 7)
            def _():
                relay_copies([i])[0].wait_recv()
            start(me == 7, lambda: prev_copies(relay_k, relay_v, 4, [i]))

        forward(0)

    def take_prev():
        for c in prev_copies(k_ref, v_ref, me - 1):
            c.wait_recv()

    pl.when(behind(1))(take_prev)
    pass_on = both(jnp.logical_not(odd), behind(1), ahead(1))

    @pl.when(pass_on)
    def _():
        list_copy(2, me, list_len)[0].wait_recv()
        pick(want_in[list_len], prev_k, prev_v, send_k.at[far], send_v.at[far])
    start(pass_on, lambda: block_copies(2, me + 1, far))

    @pl.when(behind(1))
    def _():
        absorb(lambda c: prev_k[:, c], lambda c: prev_v[:, c], top_l, sum_l, acc_l)
        pick(want_out[0], prev_k, prev_v, mem_k.at[0], mem_v.at[0])

    if detour:
        for i in range(1, 4):
            forward(i)

        @pl.when(me == 7)
        def _():
            list_copy(3, 6)[0].wait_recv()
            pick(want_in[2], relay_k, relay_v, send_k.at[1], send_v.at[1])
            pick(want_out[3], relay_k, relay_v, mem_k.at[3], mem_v.at[3])
        start(me == 7, lambda: block_copies(3, 6))

    for low, high in GROUPS:
        for d in range(max(low, 2), min(high, list_len) + 1):
            @pl.when(both(behind(d), me != 7) if detour and d == 4 else behind(d))
            def _():
                for c in block_copies(d, me - d):
                    c.wait_recv()

        @pl.when(behind(low))
        def _():
            last = min(high, list_len)

            def load(blocks):
                return lambda c: blocks[low - 1:last, :, c].reshape((last - low + 1) * BLOCK, hd)
            absorb(load(mem_k), load(mem_v), top_m, sum_m, acc_m, some_wants=wants[low - 1:last], first=low == 1)

    def finish(h, carry):
        cols = pl.ds(pl.multiple_of(h * hd, hd), hd)
        row = pl.ds(h, 1)
        gate = 1.0 / (1.0 + jnp.exp(jnp.full((1, seg), -bias_ref[h], jnp.float32)))
        mixed = (acc_m[cols, :] * (gate / jnp.maximum(sum_m[row, :], 1.0))
                 + acc_l[cols, :] * ((1.0 - gate) / jnp.maximum(sum_l[row, :], 1.0)))
        out_ref[:, cols] = mixed.T.astype(jnp.bfloat16)
        return carry

    lax.fori_loop(0, heads, finish, 0, unroll=UNROLL)

    for condition, copies in unfinished:
        @pl.when(condition)
        def _():
            for c in copies():
                c.wait_send()


ORDER = ((0, 0, 0, 0, 0, 0, 0),
         (1, 0, 0, 0, 0, 0, 0),
         (1, 0, 0, 0, 0, 0, 2),
         (1, 2, 0, 0, 0, 0, 3),
         (4, 1, 0, 0, 0, 2, 3),
         (1, 5, 2, 0, 0, 3, 4),
         (1, 3, 2, 5, 0, 6, 4),
         (1, 4, 2, 3, 6, 5, 7))
STAGES = ((0, 3), (3, 2), (5, 1), (6, 1))
HOLDERS = ((), (), (0,), (0, 2), (1, 2), (1, 2, 4), (1, 2, 4, 7), (1, 2, 4, 6))
SENDS = {0: ((2, 2, "own"), (3, 3, "own")),
         1: ((7, 6, "own"), (6, 5, "own"), (4, 3, "own"), (5, 4, "own")),
         2: ((5, 3, "own"), (4, 2, "own"), (7, 5, "own"), (6, 4, "own"), (3, 2, "prev")),
         4: ((6, 2, "own"), (7, 3, "own"), (6, 6, "aux"), (7, 7, "aux"), (5, 5, "aux"), (5, 2, "prev")),
         6: ((7, 2, "prev"),),
         7: ((6, 3, "aux"),)}
SLOTS = 6
VMEM_LIMIT = 60 * 2 ** 20


def eight(list_len, heads, q_hbm, k_hbm, v_hbm, bias_hbm, src_hbm, blk_hbm, live_hbm, out_ref,
          q_ref, k_ref, v_ref, bias_ref, src_ref, blk_ref, live_ref, load_s, prev_k, prev_v, aux_k, aux_v, mem_k, mem_v, send_k, send_v, want_out, want_in,
          top_l, sum_l, acc_l, top_m, sum_m, acc_m,
          list_ss, list_rs, prev_ss, prev_rs, aux_ss, aux_rs, blk_ss, blk_rs, turn):
    me = lax.axis_index("tm")
    seg, width = q_ref.shape
    hd = width // heads
    per_seg = seg // BLOCK
    loads = [pltpu.make_async_copy(source, target, load_s.at[i]) for i, (source, target) in enumerate(
        ((src_hbm, src_ref), (blk_hbm, blk_ref), (live_hbm, live_ref), (bias_hbm, bias_ref),
         (k_hbm, k_ref), (q_hbm, q_ref), (v_hbm, v_ref)))]
    for load in loads:
        load.start()
    barrier = pltpu.get_barrier_semaphore()
    for other in range(8):
        @pl.when(me != other)
        def _():
            pl.semaphore_signal(barrier, inc=1, device_id={"tm": other}, device_id_type=MESH)
    places = len(ORDER[0])
    slope = math.log2(math.e) / math.sqrt(hd)

    def any_of(devices):
        result = me == devices[0]
        for device in devices[1:]:
            result = jnp.logical_or(result, me == device)
        return result

    def want_of(distance):
        want = jnp.int32(-1)
        for e in range(list_len):
            hit = (live_ref[0, e] > 0) & (me - src_ref[0, e] == distance)
            want = jnp.where(hit, blk_ref[0, e], want)
        return want

    for load in loads[:3]:
        load.wait()
    wants = []
    for p in range(places):
        distance = jnp.int32(100)
        for r in range(8):
            if ORDER[r][p]:
                distance = jnp.where(me == r, ORDER[r][p], distance)
        wants.append(want_of(distance))
    row = lax.broadcasted_iota(jnp.int32, (8, 128), 0)
    tile = jnp.full((8, 128), -1, jnp.int32)
    for d in range(1, list_len + 1):
        tile = jnp.where(row == d - 1, want_of(d), tile)
    want_out[...] = tile
    pl.semaphore_wait(barrier, 7)

    def remote(source, target, send, recv, device):
        return pltpu.make_async_remote_copy(source, target, send, recv, device_id={"tm": device},
                                            device_id_type=MESH)

    def pieces(keys, values):
        half = width // 2
        return [part.at[:, pl.ds(i * half, half)] for i in range(2) for part in (keys, values)]

    def prev_copy(i, keys, values, device):
        return remote(pieces(keys, values)[i], pieces(prev_k, prev_v)[i], prev_ss.at[i], prev_rs.at[i], device)

    def aux_copy(i, device):
        return remote(pieces(k_hbm, v_hbm)[i], pieces(aux_k, aux_v)[i], aux_ss.at[i], aux_rs.at[i], device)

    def list_copy(i, slot, device):
        return remote(want_out, want_in.at[slot], list_ss.at[i], list_rs.at[slot], device)

    def block_copies(slot, place, device):
        return [remote(here.at[slot], there.at[place], blk_ss.at[i, slot], blk_rs.at[i, place], device)
                for i, (here, there) in enumerate(((send_k, mem_k), (send_v, mem_v)))]

    def pick(want, source, to_k, to_v):
        from_k, from_v = {"own": (k_ref, v_ref), "prev": (prev_k, prev_v), "aux": (aux_k, aux_v)}[source]
        ones = [jnp.where(want == b, 1.0, 0.0).astype(jnp.bfloat16) for b in range(per_seg)]

        def one_strip(h, carry):
            cols = pl.ds(pl.multiple_of(h * 128, 128), 128)
            for origin, target in ((from_k, to_k), (from_v, to_v)):
                total = origin[:BLOCK, cols] * ones[0]
                for b in range(1, per_seg):
                    total = total + origin[b * BLOCK:(b + 1) * BLOCK, cols] * ones[b]
                target[:, cols] = total
            return carry

        lax.fori_loop(0, width // 128, one_strip, 0)

    def pick_send(device, chosen):
        for slot in chosen:
            reader, distance, source = SENDS[device][slot]
            pick(want_in[reader - 2, distance - 1:distance, :], source, send_k.at[slot], send_v.at[slot])

    def start_send(device, chosen):
        for slot in chosen:
            reader, distance, source = SENDS[device][slot]
            for c in block_copies(slot, ORDER[reader].index(distance), reader):
                c.start()

    def pick_own(place, source):
        pick(jnp.full((1, 128), wants[place], jnp.int32), source, mem_k.at[place], mem_v.at[place])

    @pl.when(me == 3)
    def _():
        for i in range(4):
            aux_copy(i, 7).start()

    @pl.when(me == 0)
    def _():
        for i in range(4):
            aux_copy(i, 4).start()
    for r in range(2, 8):
        @pl.when(me == r)
        def _():
            for i, holder in enumerate(HOLDERS[r]):
                list_copy(i, r - 2, holder).start()
    gives = any_of((0, 1, 2, 4, 5, 6))

    @pl.when(gives)
    def _():
        for i in range(4):
            prev_copy(i, k_hbm, v_hbm, me + 1).start()

    for load in loads[3:]:
        load.wait()

    for device in (0, 1, 2, 4, 6, 7):
        @pl.when(me == device)
        def _():
            for r in range(2, 8):
                if device in HOLDERS[r]:
                    list_copy(0, r - 2, r).wait_recv()
            pick_send(device, [i for i, entry in enumerate(SENDS[device]) if entry[2] == "own"])
            if device == 1:
                start_send(1, (0, 1))

    for devices, place in (((1, 2), 1), ((1, 2, 3, 4), 2), ((6,), 4)):
        @pl.when(any_of(devices))
        def _():
            mem_k[place] = jnp.zeros((BLOCK, width), jnp.bfloat16)
            mem_v[place] = jnp.zeros((BLOCK, width), jnp.bfloat16)

    def absorb(load_k, load_v, top, total, acc, some_wants=None, causal=False, first=False):
        lives = None if some_wants is None else [jnp.full((1, seg), w, jnp.int32) >= 0 for w in some_wants]

        def one_head(h, carry):
            cols = pl.ds(pl.multiple_of(h * hd, hd), hd)
            row = pl.ds(h, 1)
            s = lax.dot_general(load_k(cols), q_ref[:, cols], (((1,), (1,)), ((), ())),
                                preferred_element_type=jnp.float32)
            if causal:
                key_at = lax.broadcasted_iota(jnp.int32, s.shape, 0)
                query_at = lax.broadcasted_iota(jnp.int32, s.shape, 1)
                s = jnp.where(key_at <= query_at, s, MASKED)
            new = None if first else top[row, :]
            if lives is None:
                high = jnp.max(s, axis=0, keepdims=True)
                new = high if first else jnp.maximum(new, high)
                p = jnp.exp2((s - new) * slope)
            else:
                strips = [s[i * BLOCK:(i + 1) * BLOCK] for i in range(len(lives))]
                for strip, live in zip(strips, lives):
                    high = jnp.where(live, jnp.max(strip, axis=0, keepdims=True), FLOOR)
                    new = high if new is None else jnp.maximum(new, high)
                p = jnp.concatenate([jnp.exp2((strip - jnp.where(live, new, BARRED)) * slope)
                                     for strip, live in zip(strips, lives)], axis=0)
            part = jnp.sum(p, axis=0, keepdims=True)
            mixed = lax.dot_general(load_v(cols), p.astype(jnp.bfloat16), (((0,), (0,)), ((), ())),
                                    preferred_element_type=jnp.float32)
            if first:
                total[row, :] = part
                acc[cols, :] = mixed
            else:
                shrink = jnp.exp2((top[row, :] - new) * slope)
                total[row, :] = total[row, :] * shrink + part
                acc[cols, :] = acc[cols, :] * shrink + mixed
            top[row, :] = new
            return carry

        lax.fori_loop(0, heads, one_head, 0, unroll=UNROLL)

    @pl.when(me == 0)
    def _():
        sum_m[...] = jnp.zeros_like(sum_m)
        acc_m[...] = jnp.zeros_like(acc_m)

    absorb(lambda c: k_ref[:, c], lambda c: v_ref[:, c], top_l, sum_l, acc_l, causal=True, first=True)

    def forward(i):
        @pl.when(me == 7)
        def _():
            aux_copy(i, 3).wait_recv()
            prev_copy(i, aux_k, aux_v, 4).start()

    def take_prev(chosen):
        for i in chosen:
            prev_copy(i, k_hbm, v_hbm, 0).wait_recv()

    def take_aux(chosen):
        for i in chosen:
            aux_copy(i, 0).wait_recv()

    forward(0)

    @pl.when(me == 2)
    def _():
        take_prev(range(4))
        start_send(2, (0, 1, 2, 3))

    @pl.when(me == 4)
    def _():
        take_aux(range(3))
        start_send(4, (0, 1))
        take_aux([3])
        pick_send(4, (2, 3, 4))
        start_send(4, (2, 3, 4))
        pick_own(0, "aux")

    @pl.when(me == 2)
    def _():
        pick_send(2, [4])
        start_send(2, [4])

    @pl.when(any_of((1, 3, 4, 5, 6, 7)))
    def _():
        take_prev(range(4))

    @pl.when(me == 4)
    def _():
        pick_send(4, [5])
        start_send(4, [5])
        pick_own(1, "prev")

    @pl.when(me == 6)
    def _():
        pick_send(6, [0])
        start_send(6, [0])

    @pl.when(any_of((1, 2, 3, 5, 6, 7)))
    def _():
        pick_own(0, "prev")

    @pl.when(me >= 1)
    def _():
        absorb(lambda c: prev_k[:, c], lambda c: prev_v[:, c], top_l, sum_l, acc_l)

    @pl.when(me == 1)
    def _():
        for i in range(4):
            prev_copy(i, k_hbm, v_hbm, 2).wait_send()
        start_send(1, (2, 3))
        for slot in (0, 1):
            for c in block_copies(slot, 0, 2):
                c.wait_send()
        pl.semaphore_signal(turn, inc=1, device_id={"tm": 0}, device_id_type=MESH)

    @pl.when(me == 0)
    def _():
        pl.semaphore_wait(turn, 1)
        start_send(0, (0, 1))

    for i in range(1, 4):
        forward(i)

    @pl.when(me == 7)
    def _():
        pick_send(7, [0])
        start_send(7, [0])
        pick_own(1, "aux")

    remote_places = {r: [] for r in range(8)}
    for device, entries in SENDS.items():
        for reader, distance, source in entries:
            remote_places[reader].append(ORDER[reader].index(distance))

    for low, count in STAGES:
        for place in range(low, low + count):
            readers = [r for r in range(8) if place in remote_places[r]]
            if readers:
                @pl.when(any_of(readers))
                def _():
                    for c in block_copies(0, place, 0):
                        c.wait_recv()
        users = [r for r in range(8) if any(ORDER[r][low:low + count])]

        @pl.when(any_of(users))
        def _():
            def load(blocks):
                return lambda c: blocks[low:low + count, :, c].reshape(count * BLOCK, hd)
            absorb(load(mem_k), load(mem_v), top_m, sum_m, acc_m, some_wants=wants[low:low + count],
                   first=low == 0)

    def finish(h, carry):
        cols = pl.ds(pl.multiple_of(h * hd, hd), hd)
        row = pl.ds(h, 1)
        gate = 1.0 / (1.0 + jnp.exp(jnp.full((1, seg), -bias_ref[h], jnp.float32)))
        mixed = (acc_m[cols, :] * (gate / jnp.maximum(sum_m[row, :], 1.0))
                 + acc_l[cols, :] * ((1.0 - gate) / jnp.maximum(sum_l[row, :], 1.0)))
        out_ref[:, cols] = mixed.T.astype(jnp.bfloat16)
        return carry

    lax.fori_loop(0, heads, finish, 0, unroll=UNROLL)

    for device in range(8):
        @pl.when(me == device)
        def _():
            for i in range(len(HOLDERS[device])):
                list_copy(i, 0, 0).wait_send()
            for slot in range(2 if device == 1 else 0, len(SENDS.get(device, ()))):
                for c in block_copies(slot, 0, 0):
                    c.wait_send()
            if device in (0, 3):
                for i in range(4):
                    aux_copy(i, 4).wait_send()
            if device not in (1, 3):
                for i in range(4):
                    prev_copy(i, k_hbm, v_hbm, 2).wait_send()


def general(n, q_proj, k_proj, v_proj, gate_bias, src_shard, src_block, valid):
    seg, width = q_proj.shape
    heads = gate_bias.shape[0]
    list_len = src_shard.shape[1]
    far = list_len - 1
    vmem = pl.BlockSpec(memory_space=pltpu.VMEM)
    smem = pl.BlockSpec(memory_space=pltpu.SMEM)
    return pl.pallas_call(
        functools.partial(kernel, n, list_len, heads),
        out_shape=jax.ShapeDtypeStruct((seg, width), jnp.bfloat16),
        in_specs=[vmem] * 3 + [smem] * 4,
        out_specs=vmem,
        scratch_shapes=[
            pltpu.VMEM((seg, width), jnp.bfloat16),
            pltpu.VMEM((seg, width), jnp.bfloat16),
            pltpu.VMEM((list_len, BLOCK, width), jnp.bfloat16),
            pltpu.VMEM((list_len, BLOCK, width), jnp.bfloat16),
            pltpu.VMEM((far + 1, BLOCK, width), jnp.bfloat16),
            pltpu.VMEM((far + 1, BLOCK, width), jnp.bfloat16),
            pltpu.VMEM((list_len, 8, 128), jnp.int32),
            pltpu.VMEM((list_len + 1, 8, 128), jnp.int32),
            pltpu.VMEM((heads, seg), jnp.float32),
            pltpu.VMEM((heads, seg), jnp.float32),
            pltpu.VMEM((width, seg), jnp.float32),
            pltpu.VMEM((heads, seg), jnp.float32),
            pltpu.VMEM((heads, seg), jnp.float32),
            pltpu.VMEM((width, seg), jnp.float32),
            pltpu.VMEM((seg, width), jnp.bfloat16),
            pltpu.VMEM((seg, width), jnp.bfloat16),
            pltpu.VMEM((BLOCK, width), jnp.bfloat16),
            pltpu.VMEM((BLOCK, width), jnp.bfloat16),
            pltpu.SemaphoreType.DMA((list_len,)),
            pltpu.SemaphoreType.DMA((list_len + 1,)),
            pltpu.SemaphoreType.DMA((4,)),
            pltpu.SemaphoreType.DMA((4,)),
            pltpu.SemaphoreType.DMA((2, far + 1)),
            pltpu.SemaphoreType.DMA((2, far)),
            pltpu.SemaphoreType.DMA((4,)),
            pltpu.SemaphoreType.DMA((4,)),
            pltpu.SemaphoreType.DMA((2,)),
            pltpu.SemaphoreType.DMA((2,)),
        ],
        compiler_params=pltpu.CompilerParams(collective_id=0, has_side_effects=True),
    )(q_proj, k_proj, v_proj, gate_bias, src_shard, src_block, valid)


def shards(n, q_proj, k_proj, v_proj, gate_bias, src_shard, src_block, valid):
    seg, width = q_proj.shape
    heads = gate_bias.shape[0]
    list_len = src_shard.shape[1]
    vmem = pl.BlockSpec(memory_space=pltpu.VMEM)
    if n != 8:
        return general(n, q_proj, k_proj, v_proj, gate_bias, src_shard, src_block, valid)
    whole = pltpu.VMEM((seg, width), jnp.bfloat16)
    return pl.pallas_call(
        functools.partial(eight, list_len, heads),
        out_shape=jax.ShapeDtypeStruct((seg, width), jnp.bfloat16),
        in_specs=[pl.BlockSpec(memory_space=pltpu.HBM)] * 7,
        out_specs=vmem,
        scratch_shapes=[whole] * 3 + [pltpu.SMEM(gate_bias.shape, jnp.float32)]
        + [pltpu.SMEM(src_shard.shape, jnp.int32)] * 3 + [pltpu.SemaphoreType.DMA((7,))] + [whole] * 4
        + [pltpu.VMEM((len(ORDER[0]), BLOCK, width), jnp.bfloat16)] * 2
        + [pltpu.VMEM((SLOTS, BLOCK, width), jnp.bfloat16)] * 2
        + [pltpu.VMEM((8, 128), jnp.int32), pltpu.VMEM((6, 8, 128), jnp.int32)]
        + [pltpu.VMEM((heads, seg), jnp.float32), pltpu.VMEM((heads, seg), jnp.float32),
           pltpu.VMEM((width, seg), jnp.float32)] * 2
        + [pltpu.SemaphoreType.DMA((4,)), pltpu.SemaphoreType.DMA((6,))]
        + [pltpu.SemaphoreType.DMA((4,))] * 4
        + [pltpu.SemaphoreType.DMA((2, SLOTS)), pltpu.SemaphoreType.DMA((2, len(ORDER[0]))),
           pltpu.SemaphoreType.REGULAR],
        compiler_params=pltpu.CompilerParams(collective_id=0, has_side_effects=True,
                                             vmem_limit_bytes=VMEM_LIMIT),
    )(q_proj, k_proj, v_proj, gate_bias, src_shard, src_block, valid)


def solution(mesh):
    rows = P(("book", "tm"), None)
    return jax.shard_map(functools.partial(shards, mesh.shape["tm"]), mesh=mesh,
                         in_specs=(rows, rows, rows, P(), rows, rows, rows), out_specs=rows, check_vma=False)
```

```python
import functools
import math

import jax
import jax.numpy as jnp
from jax import lax
from jax.experimental import pallas as pl
from jax.experimental.pallas import tpu as pltpu
from jax.sharding import PartitionSpec as P

BLOCK = 128
MASKED = -1e30
FLOOR = -1e29
BARRED = 1e30
UNROLL = 4
GROUPS = ((1, 4), (5, 7))
MESH = pl.DeviceIdType.MESH


def kernel(n, list_len, heads, q_ref, k_ref, v_ref, bias_ref, src_ref, blk_ref, live_ref, out_ref,
           prev_k, prev_v, mem_k, mem_v, send_k, send_v, want_out, want_in,
           top_l, sum_l, acc_l, top_m, sum_m, acc_m,
           relay_k, relay_v, hop_k, hop_v,
           list_ss, list_rs, prev_ss, prev_rs, blk_ss, blk_rs, relay_ss, relay_rs, hop_ss, hop_rs):
    me = lax.axis_index("tm")
    seg, width = q_ref.shape
    hd = width // heads
    per_seg = seg // BLOCK
    far = list_len - 1
    slope = math.log2(math.e) / math.sqrt(hd)

    wants = []
    for d in range(1, list_len + 1):
        want = jnp.int32(-1)
        for e in range(list_len):
            hit = (live_ref[0, e] > 0) & (me - src_ref[0, e] == d)
            want = jnp.where(hit, blk_ref[0, e], want)
        wants.append(want)
        want_out[d - 1] = jnp.full((8, 128), want, jnp.int32)

    def ahead(d):
        return me + d < n

    def behind(d):
        return me - d >= 0

    barrier = pltpu.get_barrier_semaphore()
    for d in range(1, list_len + 1):
        @pl.when(ahead(d))
        def _():
            pl.semaphore_signal(barrier, inc=1, device_id={"tm": me + d}, device_id_type=MESH)

        @pl.when(behind(d))
        def _():
            pl.semaphore_signal(barrier, inc=1, device_id={"tm": me - d}, device_id_type=MESH)
    near = jnp.minimum(me, list_len) + jnp.minimum(n - 1 - me, list_len)
    pl.semaphore_wait(barrier, near)

    detour = n == 8
    odd = lax.rem(me, 2) == 1

    def both(*conditions):
        result = conditions[0]
        for condition in conditions[1:]:
            result = jnp.logical_and(result, condition)
        return result

    def remote(source, target, send, recv, device):
        return pltpu.make_async_remote_copy(source, target, send, recv, device_id={"tm": device},
                                            device_id_type=MESH)

    unfinished = []

    def start(condition, copies):
        @pl.when(condition)
        def _():
            for c in copies():
                c.start()
        unfinished.append((condition, copies))

    def direct(source, d):
        result = both(source >= 0, source + d < n)
        if d == 2:
            result = both(result, lax.rem(source, 2) == 0)
        if detour and d in (3, 4):
            result = both(result, source != 3)
        return result

    def list_copy(d, target, slot=None):
        slot = d - 1 if slot is None else slot
        return [remote(want_out.at[d - 1], want_in.at[slot], list_ss.at[d - 1], list_rs.at[slot], target)]

    def pieces(keys, values):
        half = seg // 2
        return [part.at[pl.ds(i * half, half)] for part in (keys, values) for i in range(2)]

    def prev_copies(keys, values, target, chosen=range(4)):
        return [remote(pieces(keys, values)[i], pieces(prev_k, prev_v)[i], prev_ss.at[i], prev_rs.at[i], target)
                for i in chosen]

    def relay_copies(chosen=range(4)):
        return [remote(pieces(k_ref, v_ref)[i], pieces(relay_k, relay_v)[i], relay_ss.at[i], relay_rs.at[i], 7)
                for i in chosen]

    def block_copies(d, target, slot=None):
        slot = d - 2 if slot is None else slot
        return [remote(here.at[slot], there.at[d - 1], blk_ss.at[i, slot], blk_rs.at[i, d - 2], target)
                for i, (here, there) in enumerate(((send_k, mem_k), (send_v, mem_v)))]

    def hop_in(d):
        return [remote(here.at[d - 2], there, blk_ss.at[i, d - 2], hop_rs.at[i], d - 2)
                for i, (here, there) in enumerate(((send_k, hop_k), (send_v, hop_v)))]

    def hop_out(d):
        return [remote(here, there.at[d - 1], hop_ss.at[i], blk_rs.at[i, d - 2], d)
                for i, (here, there) in enumerate(((hop_k, mem_k), (hop_v, mem_v)))]

    def pick(want, from_k, from_v, to_k, to_v):
        ones = [jnp.where(want == b, 1.0, 0.0)[:1].astype(jnp.bfloat16) for b in range(per_seg)]

        def one_strip(h, carry):
            cols = pl.ds(pl.multiple_of(h * 128, 128), 128)
            for source, target in ((from_k, to_k), (from_v, to_v)):
                total = source[:BLOCK, cols] * ones[0]
                for b in range(1, per_seg):
                    total = total + source[b * BLOCK:(b + 1) * BLOCK, cols] * ones[b]
                target[:, cols] = total
            return carry

        lax.fori_loop(0, width // 128, one_strip, 0)

    for d in range(list_len, 1, -1):
        start(direct(me - d, d), lambda d=d: list_copy(d, me - d))
    start(both(odd, behind(2)), lambda: list_copy(2, me - 1, list_len))
    if detour:
        start(me == 6, lambda: list_copy(3, 7))
        start(me == 3, relay_copies)
        start(both(ahead(1), me != 3), lambda: prev_copies(k_ref, v_ref, me + 1))
    else:
        start(ahead(1), lambda: prev_copies(k_ref, v_ref, me + 1))

    for d in range(list_len, 1, -1):
        @pl.when(direct(me, d))
        def _():
            for c in list_copy(d, me + d):
                c.wait_recv()
            pick(want_in[d - 1], k_ref, v_ref, send_k.at[d - 2], send_v.at[d - 2])
    for d in range(list_len, 1, -1):
        if detour and d in (6, 7):
            start(me == 0, lambda d=d: hop_in(d))
            start(both(direct(me, d), me != 0), lambda d=d: block_copies(d, me + d))
        else:
            start(direct(me, d), lambda d=d: block_copies(d, me + d))

    def absorb(load_k, load_v, top, total, acc, some_wants=None, causal=False, first=False):
        lives = None if some_wants is None else [jnp.full((1, seg), w, jnp.int32) >= 0 for w in some_wants]

        def one_head(h, carry):
            cols = pl.ds(pl.multiple_of(h * hd, hd), hd)
            row = pl.ds(h, 1)
            s = lax.dot_general(load_k(cols), q_ref[:, cols], (((1,), (1,)), ((), ())),
                                preferred_element_type=jnp.float32)
            if causal:
                key_at = lax.broadcasted_iota(jnp.int32, s.shape, 0)
                query_at = lax.broadcasted_iota(jnp.int32, s.shape, 1)
                s = jnp.where(key_at <= query_at, s, MASKED)
            new = None if first else top[row, :]
            if lives is None:
                high = jnp.max(s, axis=0, keepdims=True)
                new = high if first else jnp.maximum(new, high)
                p = jnp.exp2((s - new) * slope)
            else:
                strips = [s[i * BLOCK:(i + 1) * BLOCK] for i in range(len(lives))]
                for strip, live in zip(strips, lives):
                    high = jnp.where(live, jnp.max(strip, axis=0, keepdims=True), FLOOR)
                    new = high if new is None else jnp.maximum(new, high)
                p = jnp.concatenate([jnp.exp2((strip - jnp.where(live, new, BARRED)) * slope)
                                     for strip, live in zip(strips, lives)], axis=0)
            part = jnp.sum(p, axis=0, keepdims=True)
            mixed = lax.dot_general(load_v(cols), p.astype(jnp.bfloat16), (((0,), (0,)), ((), ())),
                                    preferred_element_type=jnp.float32)
            if first:
                total[row, :] = part
                acc[cols, :] = mixed
            else:
                shrink = jnp.exp2((top[row, :] - new) * slope)
                total[row, :] = total[row, :] * shrink + part
                acc[cols, :] = acc[cols, :] * shrink + mixed
            top[row, :] = new
            return carry

        lax.fori_loop(0, heads, one_head, 0, unroll=UNROLL)

    @pl.when(jnp.logical_not(behind(1)))
    def _():
        sum_m[...] = jnp.zeros_like(sum_m)
        acc_m[...] = jnp.zeros_like(acc_m)
    for d in range(2, list_len + 1):
        @pl.when(jnp.logical_not(behind(d)))
        def _():
            mem_k[d - 1] = jnp.zeros((BLOCK, width), jnp.bfloat16)
            mem_v[d - 1] = jnp.zeros((BLOCK, width), jnp.bfloat16)

    absorb(lambda c: k_ref[:, c], lambda c: v_ref[:, c], top_l, sum_l, acc_l, causal=True, first=True)

    if detour:
        for d in (6, 7):
            @pl.when(me == d - 2)
            def _():
                for c in hop_in(d):
                    c.wait_recv()
            start(me == d - 2, lambda d=d: hop_out(d))

        def forward(i):
            @pl.when(me == 7)
            def _():
                relay_copies([i])[0].wait_recv()
            start(me == 7, lambda: prev_copies(relay_k, relay_v, 4, [i]))

        forward(0)

    def take_prev():
        for c in prev_copies(k_ref, v_ref, me - 1):
            c.wait_recv()

    pl.when(behind(1))(take_prev)
    pass_on = both(jnp.logical_not(odd), behind(1), ahead(1))

    @pl.when(pass_on)
    def _():
        list_copy(2, me, list_len)[0].wait_recv()
        pick(want_in[list_len], prev_k, prev_v, send_k.at[far], send_v.at[far])
    start(pass_on, lambda: block_copies(2, me + 1, far))

    @pl.when(behind(1))
    def _():
        absorb(lambda c: prev_k[:, c], lambda c: prev_v[:, c], top_l, sum_l, acc_l)
        pick(want_out[0], prev_k, prev_v, mem_k.at[0], mem_v.at[0])

    if detour:
        for i in range(1, 4):
            forward(i)

        @pl.when(me == 7)
        def _():
            list_copy(3, 6)[0].wait_recv()
            pick(want_in[2], relay_k, relay_v, send_k.at[1], send_v.at[1])
            pick(want_out[3], relay_k, relay_v, mem_k.at[3], mem_v.at[3])
        start(me == 7, lambda: block_copies(3, 6))

    for low, high in GROUPS:
        for d in range(max(low, 2), min(high, list_len) + 1):
            @pl.when(both(behind(d), me != 7) if detour and d == 4 else behind(d))
            def _():
                for c in block_copies(d, me - d):
                    c.wait_recv()

        @pl.when(behind(low))
        def _():
            last = min(high, list_len)

            def load(blocks):
                return lambda c: blocks[low - 1:last, :, c].reshape((last - low + 1) * BLOCK, hd)
            absorb(load(mem_k), load(mem_v), top_m, sum_m, acc_m, some_wants=wants[low - 1:last], first=low == 1)

    def finish(h, carry):
        cols = pl.ds(pl.multiple_of(h * hd, hd), hd)
        row = pl.ds(h, 1)
        gate = 1.0 / (1.0 + jnp.exp(jnp.full((1, seg), -bias_ref[h], jnp.float32)))
        mixed = (acc_m[cols, :] * (gate / jnp.maximum(sum_m[row, :], 1.0))
                 + acc_l[cols, :] * ((1.0 - gate) / jnp.maximum(sum_l[row, :], 1.0)))
        out_ref[:, cols] = mixed.T.astype(jnp.bfloat16)
        return carry

    lax.fori_loop(0, heads, finish, 0, unroll=UNROLL)

    for condition, copies in unfinished:
        @pl.when(condition)
        def _():
            for c in copies():
                c.wait_send()


ORDER = ((0, 0, 0, 0, 0, 0, 0),
         (1, 0, 0, 0, 0, 0, 0),
         (1, 0, 0, 0, 0, 0, 2),
         (1, 2, 0, 0, 0, 0, 3),
         (4, 1, 0, 0, 0, 2, 3),
         (1, 5, 2, 0, 0, 3, 4),
         (1, 3, 2, 5, 0, 6, 4),
         (1, 4, 2, 3, 6, 5, 7))
STAGES = ((0, 3), (3, 2), (5, 1), (6, 1))
HOLDERS = ((), (), (0,), (0, 2), (1, 2), (1, 2, 4), (1, 2, 4, 7), (1, 2, 4, 6))
SENDS = {0: ((2, 2, "own"), (3, 3, "own")),
         1: ((7, 6, "own"), (6, 5, "own"), (4, 3, "own"), (5, 4, "own")),
         2: ((5, 3, "own"), (4, 2, "own"), (7, 5, "own"), (6, 4, "own"), (3, 2, "prev")),
         4: ((6, 2, "own"), (7, 3, "own"), (6, 6, "aux"), (7, 7, "aux"), (5, 5, "aux"), (5, 2, "prev")),
         6: ((7, 2, "prev"),),
         7: ((6, 3, "aux"),)}
SLOTS = 6
PARTS = 2
VMEM_LIMIT = 40 * 2 ** 20


def eight(list_len, heads, q_hbm, k_hbm, v_hbm, bias_hbm, src_hbm, blk_hbm, live_hbm, out_ref,
          q_ref, k_ref, v_ref, bias_ref, src_ref, blk_ref, live_ref, load_s, prev_k, prev_v, aux_k, aux_v, mem_k, mem_v, send_k, send_v, want_out, want_in,
          top_l, sum_l, acc_l, top_m, sum_m, acc_m,
          list_ss, list_rs, prev_ss, prev_rs, aux_ss, aux_rs, blk_ss, blk_rs, turn):
    me = lax.axis_index("tm")
    seg, width = q_ref.shape
    hd = width // heads
    per_seg = seg // BLOCK
    loads = [pltpu.make_async_copy(source, target, load_s.at[i]) for i, (source, target) in enumerate(
        ((src_hbm, src_ref), (blk_hbm, blk_ref), (live_hbm, live_ref), (bias_hbm, bias_ref),
         (k_hbm, k_ref), (q_hbm, q_ref), (v_hbm, v_ref)))]
    for load in loads:
        load.start()
    barrier = pltpu.get_barrier_semaphore()
    for other in range(8):
        @pl.when(me != other)
        def _():
            pl.semaphore_signal(barrier, inc=1, device_id={"tm": other}, device_id_type=MESH)
    places = len(ORDER[0])
    slope = math.log2(math.e) / math.sqrt(hd)

    def any_of(devices):
        result = me == devices[0]
        for device in devices[1:]:
            result = jnp.logical_or(result, me == device)
        return result

    def want_of(distance):
        want = jnp.int32(-1)
        for e in range(list_len):
            hit = (live_ref[0, e] > 0) & (me - src_ref[0, e] == distance)
            want = jnp.where(hit, blk_ref[0, e], want)
        return want

    pl.semaphore_wait(barrier, 7)

    def remote(source, target, send, recv, device):
        return pltpu.make_async_remote_copy(source, target, send, recv, device_id={"tm": device},
                                            device_id_type=MESH)

    def pieces(keys, values):
        half = width // 2
        return [part.at[:, pl.ds(i * half, half)] for i in range(2) for part in (keys, values)]

    def prev_copy(i, keys, values, device):
        return remote(pieces(keys, values)[i], pieces(prev_k, prev_v)[i], prev_ss.at[i], prev_rs.at[i], device)

    def aux_copy(i, device):
        return remote(pieces(k_hbm, v_hbm)[i], pieces(aux_k, aux_v)[i], aux_ss.at[i], aux_rs.at[i], device)

    def list_copy(i, slot, device):
        return remote(want_out, want_in.at[slot], list_ss.at[i], list_rs.at[slot], device)

    def block_copies(slot, place, device):
        wide = width // PARTS
        return [remote(here.at[slot, :, pl.ds(j * wide, wide)], there.at[place, :, pl.ds(j * wide, wide)],
                       blk_ss.at[i, j, slot], blk_rs.at[i, j, place], device)
                for j in range(PARTS) for i, (here, there) in enumerate(((send_k, mem_k), (send_v, mem_v)))]

    def pick(want, source, to_k, to_v):
        from_k, from_v = {"own": (k_ref, v_ref), "prev": (prev_k, prev_v), "aux": (aux_k, aux_v)}[source]
        ones = [jnp.where(want == b, 1.0, 0.0).astype(jnp.bfloat16) for b in range(per_seg)]

        def one_strip(h, carry):
            cols = pl.ds(pl.multiple_of(h * 128, 128), 128)
            for origin, target in ((from_k, to_k), (from_v, to_v)):
                total = origin[:BLOCK, cols] * ones[0]
                for b in range(1, per_seg):
                    total = total + origin[b * BLOCK:(b + 1) * BLOCK, cols] * ones[b]
                target[:, cols] = total
            return carry

        lax.fori_loop(0, width // 128, one_strip, 0)

    def pick_send(device, chosen):
        for slot in chosen:
            reader, distance, source = SENDS[device][slot]
            pick(want_in[reader - 2, distance - 1:distance, :], source, send_k.at[slot], send_v.at[slot])

    def start_send(device, chosen):
        for slot in chosen:
            reader, distance, source = SENDS[device][slot]
            for c in block_copies(slot, ORDER[reader].index(distance), reader):
                c.start()

    def pick_own(place, source):
        pick(jnp.full((1, 128), wants[place], jnp.int32), source, mem_k.at[place], mem_v.at[place])

    def start_whole():
        for i in range(4):
            prev_copy(i, k_hbm, v_hbm, me + 1).start()

    @pl.when(me == 3)
    def _():
        for i in range(4):
            aux_copy(i, 7).start()

    @pl.when(me == 0)
    def _():
        for i in range(4):
            aux_copy(i, 4).start()
    pl.when(any_of((0, 1, 2, 4, 6)))(start_whole)

    for load in loads[:3]:
        load.wait()
    wants = []
    for p in range(places):
        distance = jnp.int32(100)
        for r in range(8):
            if ORDER[r][p]:
                distance = jnp.where(me == r, ORDER[r][p], distance)
        wants.append(want_of(distance))
    row = lax.broadcasted_iota(jnp.int32, (8, 128), 0)
    tile = jnp.full((8, 128), -1, jnp.int32)
    for d in range(1, list_len + 1):
        tile = jnp.where(row == d - 1, want_of(d), tile)
    want_out[...] = tile

    for r in range(2, 8):
        @pl.when(me == r)
        def _():
            for i, holder in enumerate(HOLDERS[r]):
                list_copy(i, r - 2, holder).start()
    pl.when(me == 5)(start_whole)

    for load in loads[3:]:
        load.wait()

    for device in (0, 1, 2, 4, 6, 7):
        @pl.when(me == device)
        def _():
            for r in range(2, 8):
                if device in HOLDERS[r]:
                    list_copy(0, r - 2, r).wait_recv()
            pick_send(device, [i for i, entry in enumerate(SENDS[device]) if entry[2] == "own"])
            if device == 1:
                start_send(1, (0, 1))

    for devices, place in (((1, 2), 1), ((1, 2, 3, 4), 2), ((6,), 4)):
        @pl.when(any_of(devices))
        def _():
            mem_k[place] = jnp.zeros((BLOCK, width), jnp.bfloat16)
            mem_v[place] = jnp.zeros((BLOCK, width), jnp.bfloat16)

    def absorb(load_k, load_v, top, total, acc, some_wants=None, causal=False, first=False,
               span=None, close=None):
        lives = None if some_wants is None else [jnp.full((1, seg), w, jnp.int32) >= 0 for w in some_wants]

        def one_head(h, carry):
            cols = pl.ds(pl.multiple_of(h * hd, hd), hd)
            row = pl.ds(h, 1)
            s = lax.dot_general(load_k(cols), q_ref[:, cols], (((1,), (1,)), ((), ())),
                                preferred_element_type=jnp.float32)
            if causal:
                key_at = lax.broadcasted_iota(jnp.int32, s.shape, 0)
                query_at = lax.broadcasted_iota(jnp.int32, s.shape, 1)
                s = jnp.where(key_at <= query_at, s, MASKED)
            new = None if first else top[row, :]
            if lives is None:
                high = jnp.max(s, axis=0, keepdims=True)
                new = high if first else jnp.maximum(new, high)
                p = jnp.exp2((s - new) * slope)
            else:
                strips = [s[i * BLOCK:(i + 1) * BLOCK] for i in range(len(lives))]
                for strip, live in zip(strips, lives):
                    high = jnp.where(live, jnp.max(strip, axis=0, keepdims=True), FLOOR)
                    new = high if new is None else jnp.maximum(new, high)
                p = jnp.concatenate([jnp.exp2((strip - jnp.where(live, new, BARRED)) * slope)
                                     for strip, live in zip(strips, lives)], axis=0)
            part = jnp.sum(p, axis=0, keepdims=True)
            mixed = lax.dot_general(load_v(cols), p.astype(jnp.bfloat16), (((0,), (0,)), ((), ())),
                                    preferred_element_type=jnp.float32)
            if close is not None:
                shrink = jnp.exp2((top[row, :] - new) * slope)
                close(h, total[row, :] * shrink + part, acc[cols, :] * shrink + mixed)
                return carry
            if first:
                total[row, :] = part
                acc[cols, :] = mixed
            else:
                shrink = jnp.exp2((top[row, :] - new) * slope)
                total[row, :] = total[row, :] * shrink + part
                acc[cols, :] = acc[cols, :] * shrink + mixed
            top[row, :] = new
            return carry

        low, high = span or (0, heads)
        lax.fori_loop(low, high, one_head, 0, unroll=min(UNROLL, high - low))

    @pl.when(me == 0)
    def _():
        sum_m[...] = jnp.zeros_like(sum_m)
        acc_m[...] = jnp.zeros_like(acc_m)

    absorb(lambda c: k_ref[:, c], lambda c: v_ref[:, c], top_l, sum_l, acc_l, causal=True, first=True)

    def forward(i):
        @pl.when(me == 7)
        def _():
            aux_copy(i, 3).wait_recv()
            prev_copy(i, aux_k, aux_v, 4).start()

    def take_prev(chosen):
        for i in chosen:
            prev_copy(i, k_hbm, v_hbm, 0).wait_recv()

    def take_aux(chosen):
        for i in chosen:
            aux_copy(i, 0).wait_recv()

    forward(0)

    @pl.when(me == 2)
    def _():
        take_prev(range(4))
        start_send(2, (0, 1, 2, 3))

    @pl.when(me == 4)
    def _():
        take_aux(range(3))
        start_send(4, (0, 1))
        take_aux([3])
        pick_send(4, (2, 3, 4))
        start_send(4, (2, 3, 4))
        pick_own(0, "aux")

    @pl.when(me == 2)
    def _():
        pick_send(2, [4])
        start_send(2, [4])

    @pl.when(any_of((1, 3, 4, 5, 6, 7)))
    def _():
        take_prev(range(4))

    @pl.when(me == 4)
    def _():
        pick_send(4, [5])
        start_send(4, [5])
        pick_own(1, "prev")

    @pl.when(me == 6)
    def _():
        pick_send(6, [0])
        start_send(6, [0])

    @pl.when(any_of((1, 2, 3, 5, 6, 7)))
    def _():
        pick_own(0, "prev")

    @pl.when(me >= 1)
    def _():
        absorb(lambda c: prev_k[:, c], lambda c: prev_v[:, c], top_l, sum_l, acc_l)

    @pl.when(me == 1)
    def _():
        for i in range(4):
            prev_copy(i, k_hbm, v_hbm, 2).wait_send()
        start_send(1, (2, 3))
        for c in block_copies(0, 0, 2) + block_copies(1, 0, 2)[:-1]:
            c.wait_send()
        pl.semaphore_signal(turn, inc=1, device_id={"tm": 0}, device_id_type=MESH)

    @pl.when(me == 0)
    def _():
        pl.semaphore_wait(turn, 1)
        start_send(0, (0, 1))

    for i in range(1, 4):
        forward(i)

    @pl.when(me == 7)
    def _():
        pick_send(7, [0])
        start_send(7, [0])
        pick_own(1, "aux")

    remote_places = {r: [] for r in range(8)}
    for device, entries in SENDS.items():
        for reader, distance, source in entries:
            remote_places[reader].append(ORDER[reader].index(distance))

    def close(h, total, acc):
        cols = pl.ds(pl.multiple_of(h * hd, hd), hd)
        row = pl.ds(h, 1)
        gate = 1.0 / (1.0 + jnp.exp(jnp.full((1, seg), -bias_ref[h], jnp.float32)))
        mixed = (acc * (gate / jnp.maximum(total, 1.0))
                 + acc_l[cols, :] * ((1.0 - gate) / jnp.maximum(sum_l[row, :], 1.0)))
        out_ref[:, cols] = mixed.T.astype(jnp.bfloat16)

    def wait_blocks(place, chosen):
        readers = [r for r in range(8) if place in remote_places[r]]
        if readers:
            @pl.when(any_of(readers))
            def _():
                for c in block_copies(0, place, 0)[chosen]:
                    c.wait_recv()

    last = len(STAGES) - 1
    for stage, (low, count) in enumerate(STAGES):
        users = [r for r in range(8) if any(ORDER[r][low:low + count])]

        def load(blocks, low=low, count=count):
            return lambda c: blocks[low:low + count, :, c].reshape(count * BLOCK, hd)

        for part in range(PARTS if stage == last else 1):
            for place in range(low, low + count):
                wait_blocks(place, slice(2 * part, 2 * part + 2) if stage == last else slice(None))

            @pl.when(any_of(users))
            def _():
                share = heads // PARTS
                ending = dict(span=(part * share, part * share + share), close=close) if stage == last else {}
                absorb(load(mem_k), load(mem_v), top_m, sum_m, acc_m, some_wants=wants[low:low + count],
                       first=low == 0, **ending)

    @pl.when(me <= 1)
    def _():
        def finish(h, carry):
            close(h, sum_m[pl.ds(h, 1), :], acc_m[pl.ds(pl.multiple_of(h * hd, hd), hd), :])
            return carry
        lax.fori_loop(0, heads, finish, 0, unroll=UNROLL)

    for device in range(8):
        @pl.when(me == device)
        def _():
            for i in range(len(HOLDERS[device])):
                list_copy(i, 0, 0).wait_send()
            sent = [c for slot in range(len(SENDS.get(device, ()))) for c in block_copies(slot, 0, 0)]
            for c in sent[4 * PARTS - 1 if device == 1 else 0:]:
                c.wait_send()
            if device in (0, 3):
                for i in range(4):
                    aux_copy(i, 4).wait_send()
            if device not in (1, 3):
                for i in range(4):
                    prev_copy(i, k_hbm, v_hbm, 2).wait_send()


def general(n, q_proj, k_proj, v_proj, gate_bias, src_shard, src_block, valid):
    seg, width = q_proj.shape
    heads = gate_bias.shape[0]
    list_len = src_shard.shape[1]
    far = list_len - 1
    vmem = pl.BlockSpec(memory_space=pltpu.VMEM)
    smem = pl.BlockSpec(memory_space=pltpu.SMEM)
    return pl.pallas_call(
        functools.partial(kernel, n, list_len, heads),
        out_shape=jax.ShapeDtypeStruct((seg, width), jnp.bfloat16),
        in_specs=[vmem] * 3 + [smem] * 4,
        out_specs=vmem,
        scratch_shapes=[
            pltpu.VMEM((seg, width), jnp.bfloat16),
            pltpu.VMEM((seg, width), jnp.bfloat16),
            pltpu.VMEM((list_len, BLOCK, width), jnp.bfloat16),
            pltpu.VMEM((list_len, BLOCK, width), jnp.bfloat16),
            pltpu.VMEM((far + 1, BLOCK, width), jnp.bfloat16),
            pltpu.VMEM((far + 1, BLOCK, width), jnp.bfloat16),
            pltpu.VMEM((list_len, 8, 128), jnp.int32),
            pltpu.VMEM((list_len + 1, 8, 128), jnp.int32),
            pltpu.VMEM((heads, seg), jnp.float32),
            pltpu.VMEM((heads, seg), jnp.float32),
            pltpu.VMEM((width, seg), jnp.float32),
            pltpu.VMEM((heads, seg), jnp.float32),
            pltpu.VMEM((heads, seg), jnp.float32),
            pltpu.VMEM((width, seg), jnp.float32),
            pltpu.VMEM((seg, width), jnp.bfloat16),
            pltpu.VMEM((seg, width), jnp.bfloat16),
            pltpu.VMEM((BLOCK, width), jnp.bfloat16),
            pltpu.VMEM((BLOCK, width), jnp.bfloat16),
            pltpu.SemaphoreType.DMA((list_len,)),
            pltpu.SemaphoreType.DMA((list_len + 1,)),
            pltpu.SemaphoreType.DMA((4,)),
            pltpu.SemaphoreType.DMA((4,)),
            pltpu.SemaphoreType.DMA((2, far + 1)),
            pltpu.SemaphoreType.DMA((2, far)),
            pltpu.SemaphoreType.DMA((4,)),
            pltpu.SemaphoreType.DMA((4,)),
            pltpu.SemaphoreType.DMA((2,)),
            pltpu.SemaphoreType.DMA((2,)),
        ],
        compiler_params=pltpu.CompilerParams(collective_id=0, has_side_effects=True),
    )(q_proj, k_proj, v_proj, gate_bias, src_shard, src_block, valid)


def shards(n, q_proj, k_proj, v_proj, gate_bias, src_shard, src_block, valid):
    seg, width = q_proj.shape
    heads = gate_bias.shape[0]
    list_len = src_shard.shape[1]
    vmem = pl.BlockSpec(memory_space=pltpu.VMEM)
    if n != 8:
        return general(n, q_proj, k_proj, v_proj, gate_bias, src_shard, src_block, valid)
    whole = pltpu.VMEM((seg, width), jnp.bfloat16)
    return pl.pallas_call(
        functools.partial(eight, list_len, heads),
        out_shape=jax.ShapeDtypeStruct((seg, width), jnp.bfloat16),
        in_specs=[pl.BlockSpec(memory_space=pltpu.HBM)] * 7,
        out_specs=vmem,
        scratch_shapes=[whole] * 3 + [pltpu.SMEM(gate_bias.shape, jnp.float32)]
        + [pltpu.SMEM(src_shard.shape, jnp.int32)] * 3 + [pltpu.SemaphoreType.DMA((7,))] + [whole] * 4
        + [pltpu.VMEM((len(ORDER[0]), BLOCK, width), jnp.bfloat16)] * 2
        + [pltpu.VMEM((SLOTS, BLOCK, width), jnp.bfloat16)] * 2
        + [pltpu.VMEM((8, 128), jnp.int32), pltpu.VMEM((6, 8, 128), jnp.int32)]
        + [pltpu.VMEM((heads, seg), jnp.float32), pltpu.VMEM((heads, seg), jnp.float32),
           pltpu.VMEM((width, seg), jnp.float32)] * 2
        + [pltpu.SemaphoreType.DMA((4,)), pltpu.SemaphoreType.DMA((6,))]
        + [pltpu.SemaphoreType.DMA((4,))] * 4
        + [pltpu.SemaphoreType.DMA((2, PARTS, SLOTS)), pltpu.SemaphoreType.DMA((2, PARTS, len(ORDER[0]))),
           pltpu.SemaphoreType.REGULAR],
        compiler_params=pltpu.CompilerParams(collective_id=0, has_side_effects=True,
                                             vmem_limit_bytes=VMEM_LIMIT),
    )(*[pltpu.with_memory_space_constraint(x, pltpu.HBM) for x in (q_proj, k_proj, v_proj, gate_bias, src_shard, src_block, valid)])


def solution(mesh):
    rows = P(("book", "tm"), None)
    return jax.shard_map(functools.partial(shards, mesh.shape["tm"]), mesh=mesh,
                         in_specs=(rows, rows, rows, P(), rows, rows, rows), out_specs=rows, check_vma=False)
```

```python
import functools
import math

import jax
import jax.numpy as jnp
from jax import lax
from jax.experimental import pallas as pl
from jax.experimental.pallas import tpu as pltpu
from jax.sharding import PartitionSpec as P

BLOCK = 128
MASKED = -1e30
FLOOR = -1e29
BARRED = 1e30
UNROLL = 4
GROUPS = ((1, 4), (5, 7))
MESH = pl.DeviceIdType.MESH


def kernel(n, list_len, heads, q_ref, k_ref, v_ref, bias_ref, src_ref, blk_ref, live_ref, out_ref,
           prev_k, prev_v, mem_k, mem_v, send_k, send_v, want_out, want_in,
           top_l, sum_l, acc_l, top_m, sum_m, acc_m,
           relay_k, relay_v, hop_k, hop_v,
           list_ss, list_rs, prev_ss, prev_rs, blk_ss, blk_rs, relay_ss, relay_rs, hop_ss, hop_rs):
    me = lax.axis_index("tm")
    seg, width = q_ref.shape
    hd = width // heads
    per_seg = seg // BLOCK
    far = list_len - 1
    slope = math.log2(math.e) / math.sqrt(hd)

    wants = []
    for d in range(1, list_len + 1):
        want = jnp.int32(-1)
        for e in range(list_len):
            hit = (live_ref[0, e] > 0) & (me - src_ref[0, e] == d)
            want = jnp.where(hit, blk_ref[0, e], want)
        wants.append(want)
        want_out[d - 1] = jnp.full((8, 128), want, jnp.int32)

    def ahead(d):
        return me + d < n

    def behind(d):
        return me - d >= 0

    barrier = pltpu.get_barrier_semaphore()
    for d in range(1, list_len + 1):
        @pl.when(ahead(d))
        def _():
            pl.semaphore_signal(barrier, inc=1, device_id={"tm": me + d}, device_id_type=MESH)

        @pl.when(behind(d))
        def _():
            pl.semaphore_signal(barrier, inc=1, device_id={"tm": me - d}, device_id_type=MESH)
    near = jnp.minimum(me, list_len) + jnp.minimum(n - 1 - me, list_len)
    pl.semaphore_wait(barrier, near)

    detour = n == 8
    odd = lax.rem(me, 2) == 1

    def both(*conditions):
        result = conditions[0]
        for condition in conditions[1:]:
            result = jnp.logical_and(result, condition)
        return result

    def remote(source, target, send, recv, device):
        return pltpu.make_async_remote_copy(source, target, send, recv, device_id={"tm": device},
                                            device_id_type=MESH)

    unfinished = []

    def start(condition, copies):
        @pl.when(condition)
        def _():
            for c in copies():
                c.start()
        unfinished.append((condition, copies))

    def direct(source, d):
        result = both(source >= 0, source + d < n)
        if d == 2:
            result = both(result, lax.rem(source, 2) == 0)
        if detour and d in (3, 4):
            result = both(result, source != 3)
        return result

    def list_copy(d, target, slot=None):
        slot = d - 1 if slot is None else slot
        return [remote(want_out.at[d - 1], want_in.at[slot], list_ss.at[d - 1], list_rs.at[slot], target)]

    def pieces(keys, values):
        half = seg // 2
        return [part.at[pl.ds(i * half, half)] for part in (keys, values) for i in range(2)]

    def prev_copies(keys, values, target, chosen=range(4)):
        return [remote(pieces(keys, values)[i], pieces(prev_k, prev_v)[i], prev_ss.at[i], prev_rs.at[i], target)
                for i in chosen]

    def relay_copies(chosen=range(4)):
        return [remote(pieces(k_ref, v_ref)[i], pieces(relay_k, relay_v)[i], relay_ss.at[i], relay_rs.at[i], 7)
                for i in chosen]

    def block_copies(d, target, slot=None):
        slot = d - 2 if slot is None else slot
        return [remote(here.at[slot], there.at[d - 1], blk_ss.at[i, slot], blk_rs.at[i, d - 2], target)
                for i, (here, there) in enumerate(((send_k, mem_k), (send_v, mem_v)))]

    def hop_in(d):
        return [remote(here.at[d - 2], there, blk_ss.at[i, d - 2], hop_rs.at[i], d - 2)
                for i, (here, there) in enumerate(((send_k, hop_k), (send_v, hop_v)))]

    def hop_out(d):
        return [remote(here, there.at[d - 1], hop_ss.at[i], blk_rs.at[i, d - 2], d)
                for i, (here, there) in enumerate(((hop_k, mem_k), (hop_v, mem_v)))]

    def pick(want, from_k, from_v, to_k, to_v):
        ones = [jnp.where(want == b, 1.0, 0.0)[:1].astype(jnp.bfloat16) for b in range(per_seg)]

        def one_strip(h, carry):
            cols = pl.ds(pl.multiple_of(h * 128, 128), 128)
            for source, target in ((from_k, to_k), (from_v, to_v)):
                total = source[:BLOCK, cols] * ones[0]
                for b in range(1, per_seg):
                    total = total + source[b * BLOCK:(b + 1) * BLOCK, cols] * ones[b]
                target[:, cols] = total
            return carry

        lax.fori_loop(0, width // 128, one_strip, 0)

    for d in range(list_len, 1, -1):
        start(direct(me - d, d), lambda d=d: list_copy(d, me - d))
    start(both(odd, behind(2)), lambda: list_copy(2, me - 1, list_len))
    if detour:
        start(me == 6, lambda: list_copy(3, 7))
        start(me == 3, relay_copies)
        start(both(ahead(1), me != 3), lambda: prev_copies(k_ref, v_ref, me + 1))
    else:
        start(ahead(1), lambda: prev_copies(k_ref, v_ref, me + 1))

    for d in range(list_len, 1, -1):
        @pl.when(direct(me, d))
        def _():
            for c in list_copy(d, me + d):
                c.wait_recv()
            pick(want_in[d - 1], k_ref, v_ref, send_k.at[d - 2], send_v.at[d - 2])
    for d in range(list_len, 1, -1):
        if detour and d in (6, 7):
            start(me == 0, lambda d=d: hop_in(d))
            start(both(direct(me, d), me != 0), lambda d=d: block_copies(d, me + d))
        else:
            start(direct(me, d), lambda d=d: block_copies(d, me + d))

    def absorb(load_k, load_v, top, total, acc, some_wants=None, causal=False, first=False):
        lives = None if some_wants is None else [jnp.full((1, seg), w, jnp.int32) >= 0 for w in some_wants]

        def one_head(h, carry):
            cols = pl.ds(pl.multiple_of(h * hd, hd), hd)
            row = pl.ds(h, 1)
            s = lax.dot_general(load_k(cols), q_ref[:, cols], (((1,), (1,)), ((), ())),
                                preferred_element_type=jnp.float32)
            if causal:
                key_at = lax.broadcasted_iota(jnp.int32, s.shape, 0)
                query_at = lax.broadcasted_iota(jnp.int32, s.shape, 1)
                s = jnp.where(key_at <= query_at, s, MASKED)
            new = None if first else top[row, :]
            if lives is None:
                high = jnp.max(s, axis=0, keepdims=True)
                new = high if first else jnp.maximum(new, high)
                p = jnp.exp2((s - new) * slope)
            else:
                strips = [s[i * BLOCK:(i + 1) * BLOCK] for i in range(len(lives))]
                for strip, live in zip(strips, lives):
                    high = jnp.where(live, jnp.max(strip, axis=0, keepdims=True), FLOOR)
                    new = high if new is None else jnp.maximum(new, high)
                p = jnp.concatenate([jnp.exp2((strip - jnp.where(live, new, BARRED)) * slope)
                                     for strip, live in zip(strips, lives)], axis=0)
            part = jnp.sum(p, axis=0, keepdims=True)
            mixed = lax.dot_general(load_v(cols), p.astype(jnp.bfloat16), (((0,), (0,)), ((), ())),
                                    preferred_element_type=jnp.float32)
            if first:
                total[row, :] = part
                acc[cols, :] = mixed
            else:
                shrink = jnp.exp2((top[row, :] - new) * slope)
                total[row, :] = total[row, :] * shrink + part
                acc[cols, :] = acc[cols, :] * shrink + mixed
            top[row, :] = new
            return carry

        lax.fori_loop(0, heads, one_head, 0, unroll=UNROLL)

    @pl.when(jnp.logical_not(behind(1)))
    def _():
        sum_m[...] = jnp.zeros_like(sum_m)
        acc_m[...] = jnp.zeros_like(acc_m)
    for d in range(2, list_len + 1):
        @pl.when(jnp.logical_not(behind(d)))
        def _():
            mem_k[d - 1] = jnp.zeros((BLOCK, width), jnp.bfloat16)
            mem_v[d - 1] = jnp.zeros((BLOCK, width), jnp.bfloat16)

    absorb(lambda c: k_ref[:, c], lambda c: v_ref[:, c], top_l, sum_l, acc_l, causal=True, first=True)

    if detour:
        for d in (6, 7):
            @pl.when(me == d - 2)
            def _():
                for c in hop_in(d):
                    c.wait_recv()
            start(me == d - 2, lambda d=d: hop_out(d))

        def forward(i):
            @pl.when(me == 7)
            def _():
                relay_copies([i])[0].wait_recv()
            start(me == 7, lambda: prev_copies(relay_k, relay_v, 4, [i]))

        forward(0)

    def take_prev():
        for c in prev_copies(k_ref, v_ref, me - 1):
            c.wait_recv()

    pl.when(behind(1))(take_prev)
    pass_on = both(jnp.logical_not(odd), behind(1), ahead(1))

    @pl.when(pass_on)
    def _():
        list_copy(2, me, list_len)[0].wait_recv()
        pick(want_in[list_len], prev_k, prev_v, send_k.at[far], send_v.at[far])
    start(pass_on, lambda: block_copies(2, me + 1, far))

    @pl.when(behind(1))
    def _():
        absorb(lambda c: prev_k[:, c], lambda c: prev_v[:, c], top_l, sum_l, acc_l)
        pick(want_out[0], prev_k, prev_v, mem_k.at[0], mem_v.at[0])

    if detour:
        for i in range(1, 4):
            forward(i)

        @pl.when(me == 7)
        def _():
            list_copy(3, 6)[0].wait_recv()
            pick(want_in[2], relay_k, relay_v, send_k.at[1], send_v.at[1])
            pick(want_out[3], relay_k, relay_v, mem_k.at[3], mem_v.at[3])
        start(me == 7, lambda: block_copies(3, 6))

    for low, high in GROUPS:
        for d in range(max(low, 2), min(high, list_len) + 1):
            @pl.when(both(behind(d), me != 7) if detour and d == 4 else behind(d))
            def _():
                for c in block_copies(d, me - d):
                    c.wait_recv()

        @pl.when(behind(low))
        def _():
            last = min(high, list_len)

            def load(blocks):
                return lambda c: blocks[low - 1:last, :, c].reshape((last - low + 1) * BLOCK, hd)
            absorb(load(mem_k), load(mem_v), top_m, sum_m, acc_m, some_wants=wants[low - 1:last], first=low == 1)

    def finish(h, carry):
        cols = pl.ds(pl.multiple_of(h * hd, hd), hd)
        row = pl.ds(h, 1)
        gate = 1.0 / (1.0 + jnp.exp(jnp.full((1, seg), -bias_ref[h], jnp.float32)))
        mixed = (acc_m[cols, :] * (gate / jnp.maximum(sum_m[row, :], 1.0))
                 + acc_l[cols, :] * ((1.0 - gate) / jnp.maximum(sum_l[row, :], 1.0)))
        out_ref[:, cols] = mixed.T.astype(jnp.bfloat16)
        return carry

    lax.fori_loop(0, heads, finish, 0, unroll=UNROLL)

    for condition, copies in unfinished:
        @pl.when(condition)
        def _():
            for c in copies():
                c.wait_send()


ORDER = ((0, 0, 0, 0, 0, 0, 0),
         (1, 0, 0, 0, 0, 0, 0),
         (1, 0, 0, 0, 0, 0, 2),
         (1, 2, 0, 0, 0, 0, 3),
         (4, 1, 0, 0, 0, 2, 3),
         (1, 5, 2, 0, 0, 3, 4),
         (1, 3, 2, 5, 0, 6, 4),
         (1, 4, 2, 3, 6, 5, 7))
STAGES = ((0, 3), (3, 2), (5, 1), (6, 1))
HOLDERS = ((), (), (0,), (0, 2), (1, 2), (1, 2, 4), (1, 2, 4, 7), (1, 2, 4, 6))
SENDS = {0: ((2, 2, "own"), (3, 3, "own")),
         1: ((7, 6, "own"), (6, 5, "own"), (4, 3, "own"), (5, 4, "own")),
         2: ((5, 3, "own"), (4, 2, "own"), (7, 5, "own"), (6, 4, "own"), (3, 2, "prev")),
         4: ((6, 2, "own"), (7, 3, "own"), (6, 6, "aux"), (7, 7, "aux"), (5, 5, "aux"), (5, 2, "prev")),
         6: ((7, 2, "prev"),),
         7: ((6, 3, "aux"),)}
SLOTS = 6
PARTS = 2
VMEM_LIMIT = 40 * 2 ** 20


def eight(list_len, heads, q_hbm, k_hbm, v_hbm, bias_hbm, src_hbm, blk_hbm, live_hbm, out_ref,
          q_ref, k_ref, v_ref, bias_ref, src_ref, blk_ref, live_ref, load_s, prev_k, prev_v, aux_k, aux_v, mem_k, mem_v, send_k, send_v, want_out, want_in,
          top_l, sum_l, acc_l, top_m, sum_m, acc_m,
          list_ss, list_rs, prev_ss, prev_rs, aux_ss, aux_rs, blk_ss, blk_rs, turn, here):
    me = lax.axis_index("tm")
    seg, width = q_ref.shape
    hd = width // heads
    per_seg = seg // BLOCK
    loads = [pltpu.make_async_copy(source, target, load_s.at[i]) for i, (source, target) in enumerate(
        ((src_hbm, src_ref), (blk_hbm, blk_ref), (live_hbm, live_ref), (bias_hbm, bias_ref),
         (k_hbm, k_ref), (q_hbm, q_ref), (v_hbm, v_ref)))]
    for load in loads:
        load.start()
    chip, core = me // 2, me % 2
    beside = [chip * 2 + 1 - core] + [other * 2 + i for other in (chip + 1 - 2 * (chip % 2), (chip + 2) % 4)
                                      for i in range(2)]

    def greet(semaphore):
        for other in beside:
            pl.semaphore_signal(semaphore, inc=1, device_id={"tm": other}, device_id_type=MESH)

    barrier = pltpu.get_barrier_semaphore()
    greet(barrier)
    places = len(ORDER[0])
    slope = math.log2(math.e) / math.sqrt(hd)

    def any_of(devices):
        result = me == devices[0]
        for device in devices[1:]:
            result = jnp.logical_or(result, me == device)
        return result

    def want_of(distance):
        want = jnp.int32(-1)
        for e in range(list_len):
            hit = (live_ref[0, e] > 0) & (me - src_ref[0, e] == distance)
            want = jnp.where(hit, blk_ref[0, e], want)
        return want

    pl.semaphore_wait(barrier, len(beside))
    greet(here)

    def remote(source, target, send, recv, device):
        return pltpu.make_async_remote_copy(source, target, send, recv, device_id={"tm": device},
                                            device_id_type=MESH)

    def pieces(keys, values):
        half = width // 2
        return [part.at[:, pl.ds(i * half, half)] for i in range(2) for part in (keys, values)]

    def prev_copy(i, keys, values, device):
        return remote(pieces(keys, values)[i], pieces(prev_k, prev_v)[i], prev_ss.at[i], prev_rs.at[i], device)

    def aux_copy(i, device):
        return remote(pieces(k_hbm, v_hbm)[i], pieces(aux_k, aux_v)[i], aux_ss.at[i], aux_rs.at[i], device)

    def list_copy(i, slot, device):
        return remote(want_out, want_in.at[slot], list_ss.at[i], list_rs.at[slot], device)

    def block_copies(slot, place, device):
        wide = width // PARTS
        return [remote(origin.at[slot, :, pl.ds(j * wide, wide)], target.at[place, :, pl.ds(j * wide, wide)],
                       blk_ss.at[i, j, slot], blk_rs.at[i, j, place], device)
                for j in range(PARTS) for i, (origin, target) in enumerate(((send_k, mem_k), (send_v, mem_v)))]

    def pick(want, source, to_k, to_v):
        from_k, from_v = {"own": (k_ref, v_ref), "prev": (prev_k, prev_v), "aux": (aux_k, aux_v)}[source]
        ones = [jnp.where(want == b, 1.0, 0.0).astype(jnp.bfloat16) for b in range(per_seg)]

        def one_strip(h, carry):
            cols = pl.ds(pl.multiple_of(h * 128, 128), 128)
            for origin, target in ((from_k, to_k), (from_v, to_v)):
                total = origin[:BLOCK, cols] * ones[0]
                for b in range(1, per_seg):
                    total = total + origin[b * BLOCK:(b + 1) * BLOCK, cols] * ones[b]
                target[:, cols] = total
            return carry

        lax.fori_loop(0, width // 128, one_strip, 0)

    def pick_send(device, chosen):
        for slot in chosen:
            reader, distance, source = SENDS[device][slot]
            pick(want_in[reader - 2, distance - 1:distance, :], source, send_k.at[slot], send_v.at[slot])

    def start_send(device, chosen):
        for slot in chosen:
            reader, distance, source = SENDS[device][slot]
            for c in block_copies(slot, ORDER[reader].index(distance), reader):
                c.start()

    def pick_own(place, source):
        pick(jnp.full((1, 128), wants[place], jnp.int32), source, mem_k.at[place], mem_v.at[place])

    def start_whole():
        for i in range(4):
            prev_copy(i, k_hbm, v_hbm, me + 1).start()

    @pl.when(me == 3)
    def _():
        for i in range(4):
            aux_copy(i, 7).start()

    @pl.when(me == 0)
    def _():
        for i in range(4):
            aux_copy(i, 4).start()
    pl.when(any_of((0, 1, 2, 4, 6)))(start_whole)

    @pl.when(me == 5)
    def _():
        prev_copy(0, k_hbm, v_hbm, me + 1).start()

    for load in loads[:3]:
        load.wait()
    wants = []
    for p in range(places):
        distance = jnp.int32(100)
        for r in range(8):
            if ORDER[r][p]:
                distance = jnp.where(me == r, ORDER[r][p], distance)
        wants.append(want_of(distance))
    row = lax.broadcasted_iota(jnp.int32, (8, 128), 0)
    tile = jnp.full((8, 128), -1, jnp.int32)
    for d in range(1, list_len + 1):
        tile = jnp.where(row == d - 1, want_of(d), tile)
    want_out[...] = tile

    pl.semaphore_wait(here, len(beside))
    for r in range(2, 8):
        @pl.when(me == r)
        def _():
            for i, holder in enumerate(HOLDERS[r]):
                list_copy(i, r - 2, holder).start()

    @pl.when(me == 5)
    def _():
        for i in range(1, 4):
            prev_copy(i, k_hbm, v_hbm, me + 1).start()

    for load in loads[3:]:
        load.wait()

    for device in (0, 1, 2, 4, 6, 7):
        @pl.when(me == device)
        def _():
            for r in range(2, 8):
                if device in HOLDERS[r]:
                    list_copy(0, r - 2, r).wait_recv()
            pick_send(device, [i for i, entry in enumerate(SENDS[device]) if entry[2] == "own"])
            if device == 1:
                start_send(1, (0, 1))

    for devices, place in (((1, 2), 1), ((1, 2, 3, 4), 2), ((6,), 4)):
        @pl.when(any_of(devices))
        def _():
            mem_k[place] = jnp.zeros((BLOCK, width), jnp.bfloat16)
            mem_v[place] = jnp.zeros((BLOCK, width), jnp.bfloat16)

    def absorb(load_k, load_v, top, total, acc, some_wants=None, causal=False, first=False,
               span=None, close=None):
        lives = None if some_wants is None else [jnp.full((1, seg), w, jnp.int32) >= 0 for w in some_wants]

        def one_head(h, carry):
            cols = pl.ds(pl.multiple_of(h * hd, hd), hd)
            row = pl.ds(h, 1)
            s = lax.dot_general(load_k(cols), q_ref[:, cols], (((1,), (1,)), ((), ())),
                                preferred_element_type=jnp.float32)
            if causal:
                key_at = lax.broadcasted_iota(jnp.int32, s.shape, 0)
                query_at = lax.broadcasted_iota(jnp.int32, s.shape, 1)
                s = jnp.where(key_at <= query_at, s, MASKED)
            new = None if first else top[row, :]
            if lives is None:
                high = jnp.max(s, axis=0, keepdims=True)
                new = high if first else jnp.maximum(new, high)
                p = jnp.exp2((s - new) * slope)
            else:
                strips = [s[i * BLOCK:(i + 1) * BLOCK] for i in range(len(lives))]
                for strip, live in zip(strips, lives):
                    high = jnp.where(live, jnp.max(strip, axis=0, keepdims=True), FLOOR)
                    new = high if new is None else jnp.maximum(new, high)
                p = jnp.concatenate([jnp.exp2((strip - jnp.where(live, new, BARRED)) * slope)
                                     for strip, live in zip(strips, lives)], axis=0)
            part = jnp.sum(p, axis=0, keepdims=True)
            mixed = lax.dot_general(load_v(cols), p.astype(jnp.bfloat16), (((0,), (0,)), ((), ())),
                                    preferred_element_type=jnp.float32)
            if close is not None:
                shrink = jnp.exp2((top[row, :] - new) * slope)
                close(h, total[row, :] * shrink + part, acc[cols, :] * shrink + mixed)
                return carry
            if first:
                total[row, :] = part
                acc[cols, :] = mixed
            else:
                shrink = jnp.exp2((top[row, :] - new) * slope)
                total[row, :] = total[row, :] * shrink + part
                acc[cols, :] = acc[cols, :] * shrink + mixed
            top[row, :] = new
            return carry

        low, high = span or (0, heads)
        lax.fori_loop(low, high, one_head, 0, unroll=min(UNROLL, high - low))

    @pl.when(me == 0)
    def _():
        sum_m[...] = jnp.zeros_like(sum_m)
        acc_m[...] = jnp.zeros_like(acc_m)

    absorb(lambda c: k_ref[:, c], lambda c: v_ref[:, c], top_l, sum_l, acc_l, causal=True, first=True)

    def forward(i):
        @pl.when(me == 7)
        def _():
            aux_copy(i, 3).wait_recv()
            prev_copy(i, aux_k, aux_v, 4).start()

    def take_prev(chosen):
        for i in chosen:
            prev_copy(i, k_hbm, v_hbm, 0).wait_recv()

    def take_aux(chosen):
        for i in chosen:
            aux_copy(i, 0).wait_recv()

    forward(0)

    @pl.when(me == 2)
    def _():
        take_prev(range(4))
        start_send(2, (0, 1, 2, 3))

    @pl.when(me == 4)
    def _():
        take_aux(range(3))
        start_send(4, (0, 1))
        take_aux([3])
        pick_send(4, (2, 3, 4))
        start_send(4, (2, 3, 4))
        pick_own(0, "aux")

    @pl.when(me == 2)
    def _():
        pick_send(2, [4])
        start_send(2, [4])

    @pl.when(any_of((1, 3, 4, 5, 6, 7)))
    def _():
        take_prev(range(4))

    @pl.when(me == 4)
    def _():
        pick_send(4, [5])
        start_send(4, [5])
        pick_own(1, "prev")

    @pl.when(me == 6)
    def _():
        pick_send(6, [0])
        start_send(6, [0])

    @pl.when(any_of((1, 2, 3, 5, 6, 7)))
    def _():
        pick_own(0, "prev")

    @pl.when(me >= 1)
    def _():
        absorb(lambda c: prev_k[:, c], lambda c: prev_v[:, c], top_l, sum_l, acc_l)

    @pl.when(me == 1)
    def _():
        for i in range(4):
            prev_copy(i, k_hbm, v_hbm, 2).wait_send()
        start_send(1, (2, 3))
        for c in block_copies(0, 0, 2) + block_copies(1, 0, 2)[:-1]:
            c.wait_send()
        pl.semaphore_signal(turn, inc=1, device_id={"tm": 0}, device_id_type=MESH)

    @pl.when(me == 0)
    def _():
        pl.semaphore_wait(turn, 1)
        start_send(0, (0, 1))

    for i in range(1, 4):
        forward(i)

    @pl.when(me == 7)
    def _():
        pick_send(7, [0])
        start_send(7, [0])
        pick_own(1, "aux")

    remote_places = {r: [] for r in range(8)}
    for device, entries in SENDS.items():
        for reader, distance, source in entries:
            remote_places[reader].append(ORDER[reader].index(distance))

    def close(h, total, acc):
        cols = pl.ds(pl.multiple_of(h * hd, hd), hd)
        row = pl.ds(h, 1)
        gate = 1.0 / (1.0 + jnp.exp(jnp.full((1, seg), -bias_ref[h], jnp.float32)))
        mixed = (acc * (gate / jnp.maximum(total, 1.0))
                 + acc_l[cols, :] * ((1.0 - gate) / jnp.maximum(sum_l[row, :], 1.0)))
        out_ref[:, cols] = mixed.T.astype(jnp.bfloat16)

    def wait_blocks(place, chosen):
        readers = [r for r in range(8) if place in remote_places[r]]
        if readers:
            @pl.when(any_of(readers))
            def _():
                for c in block_copies(0, place, 0)[chosen]:
                    c.wait_recv()

    last = len(STAGES) - 1
    for stage, (low, count) in enumerate(STAGES):
        users = [r for r in range(8) if any(ORDER[r][low:low + count])]

        def load(blocks, low=low, count=count):
            return lambda c: blocks[low:low + count, :, c].reshape(count * BLOCK, hd)

        for part in range(PARTS if stage == last else 1):
            for place in range(low, low + count):
                wait_blocks(place, slice(2 * part, 2 * part + 2) if stage == last else slice(None))

            @pl.when(any_of(users))
            def _():
                share = heads // PARTS
                ending = dict(span=(part * share, part * share + share), close=close) if stage == last else {}
                absorb(load(mem_k), load(mem_v), top_m, sum_m, acc_m, some_wants=wants[low:low + count],
                       first=low == 0, **ending)

    @pl.when(me <= 1)
    def _():
        def finish(h, carry):
            close(h, sum_m[pl.ds(h, 1), :], acc_m[pl.ds(pl.multiple_of(h * hd, hd), hd), :])
            return carry
        lax.fori_loop(0, heads, finish, 0, unroll=UNROLL)

    for device in range(8):
        @pl.when(me == device)
        def _():
            for i in range(len(HOLDERS[device])):
                list_copy(i, 0, 0).wait_send()
            sent = [c for slot in range(len(SENDS.get(device, ()))) for c in block_copies(slot, 0, 0)]
            for c in sent[4 * PARTS - 1 if device == 1 else 0:]:
                c.wait_send()
            if device in (0, 3):
                for i in range(4):
                    aux_copy(i, 4).wait_send()
            if device not in (1, 3):
                for i in range(4):
                    prev_copy(i, k_hbm, v_hbm, 2).wait_send()


def general(n, q_proj, k_proj, v_proj, gate_bias, src_shard, src_block, valid):
    seg, width = q_proj.shape
    heads = gate_bias.shape[0]
    list_len = src_shard.shape[1]
    far = list_len - 1
    vmem = pl.BlockSpec(memory_space=pltpu.VMEM)
    smem = pl.BlockSpec(memory_space=pltpu.SMEM)
    return pl.pallas_call(
        functools.partial(kernel, n, list_len, heads),
        out_shape=jax.ShapeDtypeStruct((seg, width), jnp.bfloat16),
        in_specs=[vmem] * 3 + [smem] * 4,
        out_specs=vmem,
        scratch_shapes=[
            pltpu.VMEM((seg, width), jnp.bfloat16),
            pltpu.VMEM((seg, width), jnp.bfloat16),
            pltpu.VMEM((list_len, BLOCK, width), jnp.bfloat16),
            pltpu.VMEM((list_len, BLOCK, width), jnp.bfloat16),
            pltpu.VMEM((far + 1, BLOCK, width), jnp.bfloat16),
            pltpu.VMEM((far + 1, BLOCK, width), jnp.bfloat16),
            pltpu.VMEM((list_len, 8, 128), jnp.int32),
            pltpu.VMEM((list_len + 1, 8, 128), jnp.int32),
            pltpu.VMEM((heads, seg), jnp.float32),
            pltpu.VMEM((heads, seg), jnp.float32),
            pltpu.VMEM((width, seg), jnp.float32),
            pltpu.VMEM((heads, seg), jnp.float32),
            pltpu.VMEM((heads, seg), jnp.float32),
            pltpu.VMEM((width, seg), jnp.float32),
            pltpu.VMEM((seg, width), jnp.bfloat16),
            pltpu.VMEM((seg, width), jnp.bfloat16),
            pltpu.VMEM((BLOCK, width), jnp.bfloat16),
            pltpu.VMEM((BLOCK, width), jnp.bfloat16),
            pltpu.SemaphoreType.DMA((list_len,)),
            pltpu.SemaphoreType.DMA((list_len + 1,)),
            pltpu.SemaphoreType.DMA((4,)),
            pltpu.SemaphoreType.DMA((4,)),
            pltpu.SemaphoreType.DMA((2, far + 1)),
            pltpu.SemaphoreType.DMA((2, far)),
            pltpu.SemaphoreType.DMA((4,)),
            pltpu.SemaphoreType.DMA((4,)),
            pltpu.SemaphoreType.DMA((2,)),
            pltpu.SemaphoreType.DMA((2,)),
        ],
        compiler_params=pltpu.CompilerParams(collective_id=0, has_side_effects=True),
    )(q_proj, k_proj, v_proj, gate_bias, src_shard, src_block, valid)


def shards(n, q_proj, k_proj, v_proj, gate_bias, src_shard, src_block, valid):
    seg, width = q_proj.shape
    heads = gate_bias.shape[0]
    list_len = src_shard.shape[1]
    vmem = pl.BlockSpec(memory_space=pltpu.VMEM)
    if n != 8:
        return general(n, q_proj, k_proj, v_proj, gate_bias, src_shard, src_block, valid)
    whole = pltpu.VMEM((seg, width), jnp.bfloat16)
    return pl.pallas_call(
        functools.partial(eight, list_len, heads),
        out_shape=jax.ShapeDtypeStruct((seg, width), jnp.bfloat16),
        in_specs=[pl.BlockSpec(memory_space=pltpu.HBM)] * 7,
        out_specs=vmem,
        scratch_shapes=[whole] * 3 + [pltpu.SMEM(gate_bias.shape, jnp.float32)]
        + [pltpu.SMEM(src_shard.shape, jnp.int32)] * 3 + [pltpu.SemaphoreType.DMA((7,))] + [whole] * 4
        + [pltpu.VMEM((len(ORDER[0]), BLOCK, width), jnp.bfloat16)] * 2
        + [pltpu.VMEM((SLOTS, BLOCK, width), jnp.bfloat16)] * 2
        + [pltpu.VMEM((8, 128), jnp.int32), pltpu.VMEM((6, 8, 128), jnp.int32)]
        + [pltpu.VMEM((heads, seg), jnp.float32), pltpu.VMEM((heads, seg), jnp.float32),
           pltpu.VMEM((width, seg), jnp.float32)] * 2
        + [pltpu.SemaphoreType.DMA((4,)), pltpu.SemaphoreType.DMA((6,))]
        + [pltpu.SemaphoreType.DMA((4,))] * 4
        + [pltpu.SemaphoreType.DMA((2, PARTS, SLOTS)), pltpu.SemaphoreType.DMA((2, PARTS, len(ORDER[0]))),
           pltpu.SemaphoreType.REGULAR, pltpu.SemaphoreType.REGULAR],
        compiler_params=pltpu.CompilerParams(collective_id=0, has_side_effects=True,
                                             vmem_limit_bytes=VMEM_LIMIT),
    )(*[pltpu.with_memory_space_constraint(x, pltpu.HBM) for x in (q_proj, k_proj, v_proj, gate_bias, src_shard, src_block, valid)])


def solution(mesh):
    rows = P(("book", "tm"), None)
    return jax.shard_map(functools.partial(shards, mesh.shape["tm"]), mesh=mesh,
                         in_specs=(rows, rows, rows, P(), rows, rows, rows), out_specs=rows, check_vma=False)
```
